32 devices in a mesh: grp: 2 (over x), seq: 16 (over z, y, core).
Axes of the slice: x: 2, y: 2, z: 4, core: 2. Of those that a mesh axis runs over, the one named last changes fastest.
Arguments:
- hidden: bfloat16 [4, 5120, 1280], P('grp', 'seq'), parts along dimension 0, may hold values from -160 to 160
- mod_shift: float32 [5120], replicated, may hold values from -3 to 3
- mod_scale: float32 [5120], replicated, may hold values from -0.5 to 0.5
- head_weight: float32 [64, 5120], replicated, may hold values from -0.078125 to 0.078125
- head_bias: float32 [64], replicated, may hold values from -3 to 3
- conv_in_weight: bfloat16 [3, 3, 3, 16, 384], replicated, may hold values from -0.3125 to 0.3125
- conv_in_bias: float32 [384], replicated, may hold values from -3 to 3
- gain_in: float32 [384], replicated, may hold values from 0.1 to 1.9
- up_weight: bfloat16 [3, 3, 384, 192], replicated, may hold values from -0.109375 to 0.109375
- up_bias: float32 [192], replicated, may hold values from -3 to 3
- gain_up: float32 [192], replicated, may hold values from 0.1 to 1.9
- out_weight: bfloat16 [3, 3, 3, 192, 96], replicated, may hold values from -0.078125 to 0.078125
- out_bias: float32 [96], replicated, may hold values from -2 to 2
Outputs:
- decoded: bfloat16 [4, 64, 320, 96], P('grp', 'seq'), parts along dimension 0
The draws below stay inside these ranges and needn't reach their ends.
There are 2 independent parts, one for each index of `grp`. The reference program is written for one: setup_inputs(seed, part) draws one part's arguments, and reference() takes and returns one part's arrays. A program takes and returns all parts, laid end to end along the dimension named above; an argument that names none is the same for every part. Nothing has to cross between parts.
All inputs are finite; a program needn't handle non-finite values.
Results may differ from the reference program's by a relative error of at most 0.0056.
Values may be sent and summed in bfloat16 or wider, within the bound.
A program may use at most 64 MiB of HBM per device.

```python
import math
import jax
import jax.numpy as jnp
from jax import lax

D = 5120
LAT = 16
C1 = 384
C2 = 192
C3 = 96
FRAMES = 2
TOK_W = 80
PATCH = 64
TOK_ROWS = 16


def draw_hidden(key, part):
    key_base = jax.random.fold_in(key, 11)
    key_rows = jax.random.fold_in(key, 12)
    key_cols = jax.random.fold_in(key, 13)
    shape_all = (FRAMES, D, TOK_ROWS * TOK_W)
    row_scale = jnp.exp(jax.random.uniform(key_rows, (FRAMES, 1, TOK_ROWS * TOK_W), minval=0.0, maxval=math.log(10.0)))
    col_jitter = jnp.exp(jax.random.uniform(key_cols, (1, D, 1), minval=0.0, maxval=math.log(2.0)))
    position = (jnp.arange(D, dtype=jnp.float32) / D).reshape(1, D, 1)
    base_vals = jnp.clip(jax.random.normal(key_base, shape_all), -4.0, 4.0)
    col_scale = 10.0 ** position * col_jitter * 0.5
    result = base_vals * row_scale * col_scale * 0.3
    return jnp.clip(result, -160.0, 160.0).astype(jnp.bfloat16)


def bell_draw(own_key, extent, deviation, reach, kind=jnp.bfloat16):
    drawn = jax.random.normal(own_key, extent, jnp.float32) * deviation
    return jnp.minimum(jnp.maximum(drawn, -reach), reach).astype(kind)


def setup_inputs(seed: int = 0, part: int = 0) -> dict:
    key_list = jax.random.split(jax.random.key(seed), 14)
    own_keys = jax.random.split(jax.random.fold_in(key_list[13], part), 14)
    return {
        "hidden": draw_hidden(jax.random.fold_in(jax.random.fold_in(key_list[13], part), 71), part),
        "mod_shift": bell_draw(key_list[1], (D,), 0.5, 3.0, jnp.float32),
        "mod_scale": jnp.clip(jax.random.uniform(key_list[2], (D,), jnp.float32, -0.5, 0.5), -0.5, 0.5),
        "head_weight": bell_draw(key_list[3], (PATCH, D), D ** -0.5, 0.078125, jnp.float32),
        "head_bias": bell_draw(key_list[4], (PATCH,), 0.5, 3.0, jnp.float32),
        "conv_in_weight": bell_draw(key_list[5], (3, 3, 3, LAT, C1), (27 * LAT) ** -0.5, 0.3125),
        "conv_in_bias": bell_draw(key_list[6], (C1,), 0.5, 3.0, jnp.float32),
        "gain_in": jnp.clip(1.0 + 0.18 * jax.random.normal(key_list[7], (C1,), jnp.float32), 0.1, 1.9),
        "up_weight": bell_draw(key_list[8], (3, 3, C1, C2), (9 * C1) ** -0.5, 0.109375),
        "up_bias": bell_draw(key_list[9], (C2,), 0.5, 3.0, jnp.float32),
        "gain_up": jnp.clip(1.0 + 0.18 * jax.random.normal(key_list[10], (C2,), jnp.float32), 0.1, 1.9),
        "out_weight": bell_draw(key_list[11], (3, 3, 3, C2, C3), (27 * C2) ** -0.5, 0.078125),
        "out_bias": bell_draw(key_list[12], (C3,), 0.3, 2.0, jnp.float32),
    }


def rms_silu(values, gain_vec):
    squares = lax.optimization_barrier(jnp.mean(values * values, axis=-1, keepdims=True))
    normed = values * lax.rsqrt(squares + 1e-06) * gain_vec
    return normed * jax.nn.sigmoid(normed)

def conv_time(values, weight):
    padded = jnp.pad(values, ((2, 0), (1, 1), (1, 1), (0, 0))).astype(jnp.float32)
    result = lax.conv_general_dilated(padded[None], weight.astype(jnp.float32), (1, 1, 1), 'VALID', dimension_numbers=('NDHWC', 'DHWIO', 'NDHWC'), precision=lax.Precision.HIGHEST)
    return result[0]

def conv_plane(values, weight):
    padded = jnp.pad(values, ((0, 0), (1, 1), (1, 1), (0, 0))).astype(jnp.float32)
    return lax.conv_general_dilated(padded, weight.astype(jnp.float32), (1, 1), 'VALID', dimension_numbers=('NHWC', 'HWIO', 'NHWC'), precision=lax.Precision.HIGHEST)

def unpatch(projected):
    frames, tok_rows, tok_cols, patch_len = projected.shape
    lat_ch = patch_len // 4
    grid = projected.reshape(frames, tok_rows, tok_cols, 2, 2, lat_ch)
    return grid.transpose(0, 1, 3, 2, 4, 5).reshape(frames, 2 * tok_rows, 2 * tok_cols, lat_ch)

def reference(hidden, mod_shift, mod_scale, head_weight, head_bias, conv_in_weight, conv_in_bias, gain_in, up_weight, up_bias, gain_up, out_weight, out_bias):
    values = hidden.astype(jnp.float32)
    token_mean = lax.optimization_barrier(jnp.mean(values, axis=1, keepdims=True))
    centred = values - token_mean
    variance = lax.optimization_barrier(jnp.mean(centred * centred, axis=1, keepdims=True))
    modded = centred * lax.rsqrt(variance + 1e-06) * (1.0 + mod_scale)[:, None] + mod_shift[:, None]
    projected = jnp.einsum('fdt,kd->ftk', modded, head_weight, precision=lax.Precision.HIGHEST) + head_bias
    projected = projected.reshape(FRAMES, TOK_ROWS, TOK_W, PATCH)
    latent = unpatch(projected.astype(jnp.bfloat16))
    first_act = rms_silu(conv_time(latent, conv_in_weight) + conv_in_bias, gain_in).astype(jnp.bfloat16)
    upsampled = jnp.repeat(jnp.repeat(first_act, 2, axis=1), 2, axis=2)
    second_act = rms_silu(conv_plane(upsampled, up_weight) + up_bias, gain_up).astype(jnp.bfloat16)
    return (conv_time(second_act, out_weight) + out_bias).astype(jnp.bfloat16)
```

```python
import functools
import math

import jax
import jax.numpy as jnp
from jax import lax
from jax.experimental import pallas as pl
from jax.experimental.pallas import tpu as pltpu
from jax.sharding import PartitionSpec as P

TOK_W = 80
HIGH = lax.Precision.HIGHEST
F32 = jnp.float32
BF16 = jnp.bfloat16


def rms_silu(values, gain_vec):
    squares = jnp.mean(values * values, axis=-1, keepdims=True)
    normed = values * lax.rsqrt(squares + 1e-06) * gain_vec
    return normed * jax.nn.sigmoid(normed)


def shift_cols(values, step):
    count = values.shape[0]
    col = lax.broadcasted_iota(jnp.int32, (count, 1), 0) % TOK_W
    if step > 0:
        return jnp.where(col == 0, 0.0, pltpu.roll(values, 1, 0))
    return jnp.where(col == TOK_W - 1, 0.0, pltpu.roll(values, count - 1, 0))


def conv_kernel(num_dev, lat_rows, chans, x_ref, w1_ref, b1_ref, g1_ref, w2_ref, b2_ref, g2_ref,
                w3_ref, b3_ref, out_ref, act1, act2, res, w1s):
    c1, c2, c3 = chans
    ch = w1_ref.shape[3]
    blank = jnp.zeros((ch, c1), BF16)
    for a in range(2):
        for b in range(3):
            for j in range(4):
                rows = slice((4 * b + j) * ch, (4 * b + j + 1) * ch)
                w1s[a, rows, 0:c1] = w1_ref[a + 1, b, j] if j < 3 else blank
                w1s[a, rows, c1 : 2 * c1] = w1_ref[a + 1, b, j - 1] if j > 0 else blank
    dev = lax.axis_index("seq")
    rows1 = lat_rows + 2
    m1 = rows1 * TOK_W
    rows2 = lat_rows + 1
    m2 = rows2 * TOK_W
    rows3 = 2 * lat_rows
    m3 = rows3 * TOK_W

    def inside(count, first, step, total):
        row = lax.broadcasted_iota(jnp.int32, (count, 1), 0) // TOK_W * step + first
        return (row >= 0) & (row < total)

    keep1 = inside(m1, dev * lat_rows - 1, 1, num_dev * lat_rows)
    for frame in range(2):
        x_now = x_ref[frame].reshape(m1, x_ref.shape[-1])
        pre = jnp.dot(x_now, w1s[1], preferred_element_type=F32)
        if frame == 1:
            x_old = x_ref[0].reshape(m1, x_ref.shape[-1])
            pre = pre + jnp.dot(x_old, w1s[0], preferred_element_type=F32)
        for r in range(2):
            val = rms_silu(pre[:, r * c1 : (r + 1) * c1] + b1_ref[...], g1_ref[...])
            val = jnp.where(keep1, val, 0.0)
            edge = shift_cols(val, 1) if r == 1 else shift_cols(val, -1)
            spot = 0 if r == 1 else 3
            act1[frame, :, :, (r + 1) * c1 : (r + 2) * c1] = val.astype(BF16).reshape(rows1, TOK_W, c1)
            act1[frame, :, :, spot * c1 : (spot + 1) * c1] = edge.astype(BF16).reshape(rows1, TOK_W, c1)

    start = (0, 1, 1, 2)
    for p in range(2):
        first = 0 if p == 0 else -1
        keep2 = inside(m2, 2 * dev * lat_rows + first, 2, 2 * num_dev * lat_rows)
        for frame in range(2):
            for s in range(4):
                q = s % 2
                lanes = slice(start[s] * c1, (start[s] + 2) * c1)
                top = act1[frame, 0:rows2, :, lanes].reshape(m2, 2 * c1)
                low = act1[frame, 1 : rows2 + 1, :, lanes].reshape(m2, 2 * c1)
                pre = jnp.dot(top, w2_ref[p, 0, q], preferred_element_type=F32)
                pre = pre + jnp.dot(low, w2_ref[p, 1, q], preferred_element_type=F32)
                val = rms_silu(pre + b2_ref[...], g2_ref[...])
                val = jnp.where(keep2, val, 0.0)
                val = jnp.concatenate([val, jnp.zeros((m2, 256 - c2), F32)], axis=1)
                pieces = [(s + 1, val)]
                if s == 3:
                    pieces.append((0, shift_cols(val, 1)))
                if s == 0:
                    pieces.append((5, shift_cols(val, -1)))
                for spot, piece in pieces:
                    piece = piece.astype(BF16).reshape(rows2, TOK_W, 256)
                    for i in range(rows2):
                        act2[frame, 2 * i + 1 - p, :, spot * 256 : (spot + 1) * 256] = piece[i]

    for s in range(4):
        lanes = slice(s * 256, (s + 3) * 256)
        old = None
        new = None
        for b in range(3):
            before = act2[0, b : b + rows3, :, lanes].reshape(m3, 768)
            after = act2[1, b : b + rows3, :, lanes].reshape(m3, 768)
            one = jnp.dot(before, w3_ref[b], preferred_element_type=F32)
            two = jnp.dot(after, w3_ref[b, :, 0:128], preferred_element_type=F32)
            old = one if old is None else old + one
            new = two if new is None else new + two
        res[pl.ds(s, m3, stride=4), :] = old[:, 0:128] + b3_ref[...]
        res[pl.ds(4 * m3 + s, m3, stride=4), :] = old[:, 128:256] + new + b3_ref[...]
    width = 4 * TOK_W
    for i in range(2 * rows3):
        out_ref[i] = jnp.transpose(res[i * width : (i + 1) * width, :])[0:c3].astype(BF16)


def exchange_kernel(num_dev, x_hbm, w_hbm, scale_hbm, shift_hbm, bias_hbm, up_hbm, outw_hbm, b1_hbm, g1_hbm, b3_hbm,
                    x1_ref, w2_ref, w3_ref, b1_ref, g1_ref, b3_ref,
                    xbuf, wbuf, modbuf, upbuf, outbuf, biasbuf, b1buf, g1buf, b3buf, send, stat, got, gotstat, rows,
                    in_sem, weight_sem, send_sem, recv_sem, stat_send, stat_recv, halo_send, halo_recv):
    frames, feat, total = x_hbm.shape
    patch, width = w_hbm.shape
    tile = total // num_dev
    half = tile // 2
    c1, c2 = up_hbm.shape[3], up_hbm.shape[2]
    c3 = outw_hbm.shape[4]
    me = lax.axis_index("seq")

    def peer(step):
        spot = me
        bit = 1
        while bit < num_dev:
            if step & bit:
                spot = spot + (1 - 2 * ((me // bit) % 2)) * bit
            bit *= 2
        return spot

    window = wbuf.shape[1]
    begin = jnp.minimum((me * feat) // 128 * 128, width - window)
    lanes = pl.ds(pl.multiple_of(begin, 128), window)
    loads = [
        pltpu.make_async_copy(w_hbm.at[:, lanes], wbuf, in_sem.at[0]),
        pltpu.make_async_copy(scale_hbm.at[:, lanes], modbuf.at[0], in_sem.at[1]),
        pltpu.make_async_copy(shift_hbm.at[:, lanes], modbuf.at[1], in_sem.at[2]),
    ]
    planes = [pltpu.make_async_copy(x_hbm.at[f], xbuf.at[f], in_sem.at[3 + f]) for f in range(frames)]
    weights = [
        pltpu.make_async_copy(up_hbm, upbuf, weight_sem.at[0]),
        pltpu.make_async_copy(outw_hbm.at[pl.ds(1, 2)], outbuf, weight_sem.at[1]),
        pltpu.make_async_copy(bias_hbm, biasbuf, weight_sem.at[2]),
        pltpu.make_async_copy(b1_hbm, b1buf, weight_sem.at[3]),
        pltpu.make_async_copy(g1_hbm, g1buf, weight_sem.at[4]),
        pltpu.make_async_copy(b3_hbm, b3buf, weight_sem.at[5]),
    ]
    for copy in loads + planes + weights:
        copy.start()

    barrier = pltpu.get_barrier_semaphore()
    for step in range(1, num_dev):
        pl.semaphore_signal(barrier, inc=1, device_id={"seq": peer(step)})

    for copy in loads:
        copy.wait()
    turn = lax.rem(begin - me * feat + window, window)
    plain = pltpu.roll(wbuf[...], turn, 1)[:, 0:feat]
    scale = pltpu.roll(jnp.broadcast_to(modbuf[0], (8, window)), turn, 1)[0:1, 0:feat]
    shift = pltpu.roll(jnp.broadcast_to(modbuf[1], (8, window)), turn, 1)[0:1, 0:feat]
    weight = plain * (1.0 + scale)
    high = weight.astype(BF16)
    low = (weight - high.astype(F32)).astype(BF16)
    stack = jnp.concatenate([high, low], axis=0)
    sums = jnp.sum(high.astype(F32) + low.astype(F32), axis=1, keepdims=True)
    base = jnp.sum(plain * shift, axis=1, keepdims=True)
    both = jnp.concatenate([sums, base], axis=0)
    line = jnp.transpose(jnp.broadcast_to(both, (2 * patch, 8)))

    def messages(f):
        out = []
        for step in range(num_dev - 1, 0, -1):
            dest = peer(step)
            out.append(pltpu.make_async_remote_copy(
                src_ref=stat.at[f, dest], dst_ref=gotstat.at[f, me], send_sem=stat_send.at[f, dest],
                recv_sem=stat_recv.at[f, me], device_id={"seq": dest}))
            out.append(pltpu.make_async_remote_copy(
                src_ref=send.at[f, dest], dst_ref=got.at[f, me], send_sem=send_sem.at[f, dest],
                recv_sem=recv_sem.at[f, me], device_id={"seq": dest}))
        return out

    def arrivals(f):
        out = []
        for step in range(num_dev - 1, 0, -1):
            origin = peer(step)
            out.append(pltpu.make_async_remote_copy(
                src_ref=stat.at[f, origin], dst_ref=gotstat.at[f, origin], send_sem=stat_send.at[f, origin],
                recv_sem=stat_recv.at[f, origin], device_id={"seq": origin}))
            out.append(pltpu.make_async_remote_copy(
                src_ref=send.at[f, origin], dst_ref=got.at[f, origin], send_sem=send_sem.at[f, origin],
                recv_sem=recv_sem.at[f, origin], device_id={"seq": origin}))
        return out

    for f in range(frames):
        planes[f].wait()
        block = xbuf[f]
        full = jnp.dot(stack, block, preferred_element_type=F32)
        values = block.astype(F32)
        mean = jnp.sum(values, axis=0, keepdims=True) * (1.0 / feat)
        centred = values - mean
        spread = jnp.sum(centred * centred, axis=0, keepdims=True)
        part = full[:patch] + full[patch:] - sums * mean
        flat = jnp.transpose(part).reshape(num_dev, 2, half, patch)
        packed = jnp.concatenate([flat[:, 0], flat[:, 1]], axis=-1)
        send[f] = packed.astype(BF16)
        for i in range(num_dev):
            stat[f, i, 0:1, 0:tile] = mean[:, i * tile : (i + 1) * tile]
            stat[f, i, 1:2, 0:tile] = spread[:, i * tile : (i + 1) * tile]
            stat[f, i, 2:3, :] = line[0:1]
            stat[f, i, 3:8, :] = jnp.zeros((5, 128), F32)
        if f == 0:
            pl.semaphore_wait(barrier, num_dev - 1)
        for copy in messages(f):
            copy.start()
        got[f, me] = send[f, me]
        gotstat[f, me] = stat[f, me]

    for copy in weights:
        copy.wait()
    taps = [[jnp.transpose(upbuf[r, c].astype(F32)) for c in range(3)] for r in range(3)]
    for p in range(2):
        for i in range(2):
            group = ((0,), (1, 2)) if p == 0 else ((0, 1), (2,))
            tall = [functools.reduce(lambda a, b: a + b, [taps[r][c] for r in group[i]]) for c in range(3)]
            for q in range(2):
                first = tall[0] if q == 0 else tall[0] + tall[1]
                second = tall[1] + tall[2] if q == 0 else tall[2]
                w2_ref[p, i, q, 0:c1, :] = first.astype(BF16)
                w2_ref[p, i, q, c1 : 2 * c1, :] = second.astype(BF16)
    w3_ref[...] = jnp.zeros(w3_ref.shape, BF16)
    b1_ref[...] = b1buf[...].reshape(1, c1)
    g1_ref[...] = g1buf[...].reshape(1, c1)
    b3_ref[...] = jnp.concatenate([b3buf[...].reshape(1, c3), jnp.zeros((1, 128 - c3), F32)], axis=1)
    for b in range(3):
        for e in range(3):
            w3_ref[b, e * 256 : e * 256 + c2, 0:c3] = outbuf[1, b, e]
            w3_ref[b, e * 256 : e * 256 + c2, 128 : 128 + c3] = outbuf[0, b, e]

    def to_next(f):
        return pltpu.make_async_remote_copy(
            src_ref=rows.at[f, 1], dst_ref=rows.at[f, 0], send_sem=halo_send.at[f, 0],
            recv_sem=halo_recv.at[f, 0], device_id={"seq": lax.rem(me + 1, num_dev)})

    def to_last(f):
        return pltpu.make_async_remote_copy(
            src_ref=rows.at[f, 1], dst_ref=rows.at[f, 2], send_sem=halo_send.at[f, 1],
            recv_sem=halo_recv.at[f, 1], device_id={"seq": lax.rem(me + num_dev - 1, num_dev)})

    for f in range(frames):
        for copy in arrivals(f):
            copy.wait_recv()
        means = gotstat[f, :, 0, :]
        off = means - jnp.mean(means, axis=0, keepdims=True)
        spread = jnp.sum(gotstat[f, :, 1, :], axis=0, keepdims=True)
        var = (spread + feat * jnp.sum(off * off, axis=0, keepdims=True)) * (1.0 / width)
        scale = jnp.transpose(jnp.broadcast_to(lax.rsqrt(var + 1e-06), (8, 128)))[0:tile, 0:1]
        lines = gotstat[f, :, 2, :]
        fixed = jnp.dot(jnp.transpose(off), lines[:, 0:patch], precision=HIGH, preferred_element_type=F32)[0:tile]
        total_base = jnp.sum(lines, axis=0, keepdims=True)[:, patch:] + biasbuf[...].reshape(1, patch)
        summed = got[f, 0].astype(F32)
        for i in range(1, num_dev):
            summed = summed + got[f, i].astype(F32)
        summed = jnp.concatenate([summed[:, :patch], summed[:, patch:]], axis=0)
        done = ((summed + fixed) * scale + total_base).astype(BF16).astype(F32)
        rows[f, 1] = jnp.concatenate([done[:half], done[half:]], axis=1).astype(BF16)

        @pl.when(me < num_dev - 1)
        def _():
            to_next(f).start()

        @pl.when(me > 0)
        def _():
            to_last(f).start()

        @pl.when(me == 0)
        def _():
            rows[f, 0] = jnp.zeros((half, 128), BF16)

        @pl.when(me == num_dev - 1)
        def _():
            rows[f, 2] = jnp.zeros((half, 128), BF16)

    ch = patch // 4
    for f in range(frames):
        @pl.when(me > 0)
        def _():
            to_next(f).wait_recv()

        @pl.when(me < num_dev - 1)
        def _():
            to_last(f).wait_recv()

        quads = []
        col = lax.broadcasted_iota(jnp.int32, (tile, 1), 0)
        for h in range(3):
            pair = rows[f, h].astype(F32)
            token = jnp.concatenate([pair[:, :patch], pair[:, patch:]], axis=0)
            before = jnp.where(col == 0, 0.0, pltpu.roll(token, 1, 0))
            after = jnp.where(col == tile - 1, 0.0, pltpu.roll(token, tile - 1, 0))
            for q in range(2):
                a = 2 * q * ch
                quads.append(jnp.concatenate(
                    [before[:, a + ch : a + 2 * ch], token[:, a : a + 2 * ch], after[:, a : a + ch]], axis=1))
        for i in range(4):
            x1_ref[f, i] = jnp.concatenate(quads[i : i + 3], axis=1).astype(BF16)

    for f in range(frames):
        for copy in messages(f):
            copy.wait_send()

        @pl.when(me < num_dev - 1)
        def _():
            to_next(f).wait_send()

        @pl.when(me > 0)
        def _():
            to_last(f).wait_send()


def local(
    hidden, mod_shift, mod_scale, head_weight, head_bias, conv_in_weight, conv_in_bias, gain_in,
    up_weight, up_bias, gain_up, out_weight, out_bias,
):
    num_dev = lax.axis_size("seq")
    frames, feat, tok_total = hidden.shape
    tile = tok_total // num_dev
    rows_dev = tile // TOK_W
    patch, width = head_weight.shape
    lat_ch, c1 = conv_in_weight.shape[3:]
    c2, c3 = out_weight.shape[3:]
    lat_rows = 2 * rows_dev
    window = min(width, (feat + 255 - math.gcd(feat, 128)) // 128 * 128)
    vmem = pl.BlockSpec(memory_space=pltpu.VMEM)
    hbm = pl.BlockSpec(memory_space=pltpu.HBM)
    half = tile // 2
    raw = (hidden, head_weight, mod_scale[None], mod_shift[None], head_bias,
           jnp.transpose(up_weight, (0, 1, 3, 2)), out_weight, conv_in_bias, gain_in, out_bias)
    x1, w2, w3, b1, g1, b3 = pl.pallas_call(
        functools.partial(exchange_kernel, num_dev),
        out_shape=[
            jax.ShapeDtypeStruct((frames, lat_rows + 2, TOK_W, 12 * lat_ch), BF16),
            jax.ShapeDtypeStruct((2, 2, 2, 2 * c1, c2), BF16),
            jax.ShapeDtypeStruct((3, 768, 256), BF16),
            jax.ShapeDtypeStruct((1, c1), F32),
            jax.ShapeDtypeStruct((1, c1), F32),
            jax.ShapeDtypeStruct((1, 128), F32),
        ],
        in_specs=[hbm] * 10,
        out_specs=[vmem] * 6,
        scratch_shapes=[
            pltpu.VMEM((frames, feat, tok_total), BF16),
            pltpu.VMEM((patch, window), F32),
            pltpu.VMEM((2, 1, window), F32),
            pltpu.VMEM((3, 3, c2, c1), BF16),
            pltpu.VMEM((2, 3, 3, c2, c3), BF16),
            pltpu.VMEM((patch,), F32),
            pltpu.VMEM((c1,), F32),
            pltpu.VMEM((c1,), F32),
            pltpu.VMEM((c3,), F32),
            pltpu.VMEM((frames, num_dev, half, 2 * patch), BF16),
            pltpu.VMEM((frames, num_dev, 8, 128), F32),
            pltpu.VMEM((frames, num_dev, half, 2 * patch), BF16),
            pltpu.VMEM((frames, num_dev, 8, 128), F32),
            pltpu.VMEM((frames, 3, half, 2 * patch), BF16),
            pltpu.SemaphoreType.DMA((5,)),
            pltpu.SemaphoreType.DMA((6,)),
            pltpu.SemaphoreType.DMA((frames, num_dev)),
            pltpu.SemaphoreType.DMA((frames, num_dev)),
            pltpu.SemaphoreType.DMA((frames, num_dev)),
            pltpu.SemaphoreType.DMA((frames, num_dev)),
            pltpu.SemaphoreType.DMA((frames, 2)),
            pltpu.SemaphoreType.DMA((frames, 2)),
        ],
        compiler_params=pltpu.CompilerParams(
            vmem_limit_bytes=24 * 1024 * 1024, collective_id=0, has_side_effects=True),
    )(*[pltpu.with_memory_space_constraint(value, pltpu.HBM) for value in raw])
    cells = frames * 2 * lat_rows * 4 * TOK_W
    out = pl.pallas_call(
        functools.partial(conv_kernel, num_dev, lat_rows, (c1, c2, c3)),
        out_shape=jax.ShapeDtypeStruct((frames * 2 * lat_rows, c3, 4 * TOK_W), BF16),
        in_specs=[vmem] * 9,
        out_specs=vmem,
        scratch_shapes=[
            pltpu.VMEM((frames, lat_rows + 2, TOK_W, 4 * c1), BF16),
            pltpu.VMEM((frames, 2 * lat_rows + 2, TOK_W, 6 * 256), BF16),
            pltpu.VMEM((cells, 128), F32),
            pltpu.VMEM((2, 12 * lat_ch, 2 * c1), BF16),
        ],
        compiler_params=pltpu.CompilerParams(vmem_limit_bytes=24 * 1024 * 1024),
    )(x1, conv_in_weight, b1, g1,
      w2, up_bias[None], gain_up[None], w3, b3)
    return out.reshape(frames, 2 * lat_rows, c3, 4 * TOK_W).transpose(0, 1, 3, 2)


def solution(mesh):
    placed = (P("grp", "seq", None), P(), P(), P(), P(), P(), P(), P(), P(), P(), P(), P(), P())
    return jax.shard_map(
        local, mesh=mesh, in_specs=placed, out_specs=P("grp", "seq", None, None), check_vma=False
    )
```

```python
import functools
import math

import jax
import jax.numpy as jnp
from jax import lax
from jax.experimental import pallas as pl
from jax.experimental.pallas import tpu as pltpu
from jax.sharding import PartitionSpec as P

TOK_W = 80
HIGH = lax.Precision.HIGHEST
F32 = jnp.float32
BF16 = jnp.bfloat16


def rms_silu(values, gain_vec):
    squares = jnp.mean(values * values, axis=-1, keepdims=True)
    normed = values * lax.rsqrt(squares + 1e-06) * gain_vec
    return normed * jax.nn.sigmoid(normed)


def shift_cols(values, step):
    count = values.shape[0]
    col = lax.broadcasted_iota(jnp.int32, (count, 1), 0) % TOK_W
    if step > 0:
        return jnp.where(col == 0, 0.0, pltpu.roll(values, 1, 0))
    return jnp.where(col == TOK_W - 1, 0.0, pltpu.roll(values, count - 1, 0))


def inside(count, first, step, total):
    row = lax.broadcasted_iota(jnp.int32, (count, 1), 0) // TOK_W * step + first
    return (row >= 0) & (row < total)


def stage_in(num_dev, dev, frame, x_ref, w1s, b1_ref, g1_ref, act1):
    rows1 = x_ref.shape[1]
    lat_rows = rows1 - 2
    c1 = g1_ref.shape[1]
    m1 = rows1 * TOK_W
    keep1 = inside(m1, dev * lat_rows - 1, 1, num_dev * lat_rows)
    x_now = x_ref[frame].reshape(m1, x_ref.shape[-1])
    pre = jnp.dot(x_now, w1s[1], preferred_element_type=F32)
    if frame == 1:
        x_old = x_ref[0].reshape(m1, x_ref.shape[-1])
        pre = pre + jnp.dot(x_old, w1s[0], preferred_element_type=F32)
    for r in range(2):
        val = rms_silu(pre[:, r * c1 : (r + 1) * c1] + b1_ref[...], g1_ref[...])
        val = jnp.where(keep1, val, 0.0)
        edge = shift_cols(val, 1) if r == 1 else shift_cols(val, -1)
        spot = 0 if r == 1 else 3
        act1[:, :, (r + 1) * c1 : (r + 2) * c1] = val.astype(BF16).reshape(rows1, TOK_W, c1)
        act1[:, :, spot * c1 : (spot + 1) * c1] = edge.astype(BF16).reshape(rows1, TOK_W, c1)


def stage_up(num_dev, dev, act1, w2_ref, b2_ref, g2_ref, act2):
    rows2 = act1.shape[0] - 1
    lat_rows = rows2 - 1
    c1 = act1.shape[2] // 4
    c2 = g2_ref.shape[1]
    m2 = rows2 * TOK_W
    start = (0, 1, 1, 2)
    for p in range(2):
        first = 0 if p == 0 else -1
        keep2 = inside(m2, 2 * dev * lat_rows + first, 2, 2 * num_dev * lat_rows)
        for s in range(4):
            q = s % 2
            lanes = slice(start[s] * c1, (start[s] + 2) * c1)
            top = act1[0:rows2, :, lanes].reshape(m2, 2 * c1)
            low = act1[1 : rows2 + 1, :, lanes].reshape(m2, 2 * c1)
            pre = jnp.dot(top, w2_ref[p, 0, q], preferred_element_type=F32)
            pre = pre + jnp.dot(low, w2_ref[p, 1, q], preferred_element_type=F32)
            val = rms_silu(pre + b2_ref[...], g2_ref[...])
            val = jnp.where(keep2, val, 0.0)
            val = jnp.concatenate([val, jnp.zeros((m2, 256 - c2), F32)], axis=1)
            pieces = [(s + 1, val)]
            if s == 3:
                pieces.append((0, shift_cols(val, 1)))
            if s == 0:
                pieces.append((5, shift_cols(val, -1)))
            for spot, piece in pieces:
                piece = piece.astype(BF16).reshape(rows2, TOK_W, 256)
                for i in range(rows2):
                    act2[2 * i + 1 - p, :, spot * 256 : (spot + 1) * 256] = piece[i]


def stage_out(act2, w3_ref, part, s):
    rows3 = act2.shape[0] - 2
    lanes = slice(s * 256, (s + 3) * 256)
    total = None
    for b in range(3):
        block = act2[b : b + rows3, :, lanes].reshape(rows3 * TOK_W, 768)
        one = jnp.dot(block, w3_ref[b, :, part], preferred_element_type=F32)
        total = one if total is None else total + one
    return total


def conv_kernel(num_dev, x_ref, w1s, b1_ref, g1_ref, w2_ref, b2_ref, g2_ref, w3_ref, res_ref, out_hbm,
                act1, act2, res, obuf, out_sem):
    dev = lax.axis_index("seq")
    rows3 = act2.shape[0] - 2
    m3 = rows3 * TOK_W
    c3 = obuf.shape[1]
    width = 4 * TOK_W
    copies = [pltpu.make_async_copy(obuf.at[i], out_hbm.at[i], out_sem.at[i]) for i in range(2 * rows3)]
    stage_in(num_dev, dev, 1, x_ref, w1s, b1_ref, g1_ref, act1)
    for i in range(rows3):
        obuf[i] = jnp.transpose(res_ref[i * width : (i + 1) * width, :])[0:c3].astype(BF16)
        copies[i].start()
    stage_up(num_dev, dev, act1, w2_ref, b2_ref, g2_ref, act2)
    for s in range(4):
        new = stage_out(act2, w3_ref, slice(0, 128), s)
        res[pl.ds(s, m3, stride=4), :] = new + res_ref[pl.ds(4 * m3 + s, m3, stride=4), :]
    for i in range(rows3):
        obuf[rows3 + i] = jnp.transpose(res[i * width : (i + 1) * width, :])[0:c3].astype(BF16)
        copies[rows3 + i].start()
    for copy in copies:
        copy.wait()


def exchange_kernel(num_dev, x_hbm, w_hbm, scale_hbm, shift_hbm, bias_hbm, up_hbm, outw_hbm, w1_hbm,
                    b1_hbm, g1_hbm, b2_hbm, g2_hbm, b3_hbm,
                    x1_ref, w1s, w2_ref, w3_ref, b1_ref, g1_ref, b2_ref, g2_ref, res_ref,
                    xbuf, wbuf, modbuf, upbuf, outbuf, w1buf, biasbuf, b1buf, g1buf, b2buf, g2buf, b3buf, act1, act2, pair, pairstat, gotpair, gotpairstat, send, stat, got, gotstat, rows,
                    in_sem, weight_sem, pair_send, pair_recv, send_sem, recv_sem, stat_send, stat_recv, halo_send, halo_recv):
    frames, feat, total = x_hbm.shape
    patch, width = w_hbm.shape
    tile = total // num_dev
    half = tile // 2
    c1, c2 = up_hbm.shape[3], up_hbm.shape[2]
    c3 = outw_hbm.shape[4]
    me = lax.axis_index("seq")

    def peer(step):
        spot = me
        bit = 1
        while bit < num_dev:
            if step & bit:
                spot = spot + (1 - 2 * ((me // bit) % 2)) * bit
            bit *= 2
        return spot

    window = wbuf.shape[1]
    begin = jnp.minimum((me * feat) // 128 * 128, width - window)
    lanes = pl.ds(pl.multiple_of(begin, 128), window)
    loads = [
        pltpu.make_async_copy(w_hbm.at[:, lanes], wbuf, in_sem.at[0]),
        pltpu.make_async_copy(scale_hbm.at[:, lanes], modbuf.at[0], in_sem.at[1]),
        pltpu.make_async_copy(shift_hbm.at[:, lanes], modbuf.at[1], in_sem.at[2]),
    ]
    planes = [pltpu.make_async_copy(x_hbm.at[f], xbuf.at[f], in_sem.at[3 + f]) for f in range(frames)]
    weights = [
        pltpu.make_async_copy(up_hbm, upbuf, weight_sem.at[0]),
        pltpu.make_async_copy(outw_hbm.at[pl.ds(1, 2)], outbuf, weight_sem.at[1]),
        pltpu.make_async_copy(bias_hbm, biasbuf, weight_sem.at[2]),
        pltpu.make_async_copy(b1_hbm, b1buf, weight_sem.at[3]),
        pltpu.make_async_copy(g1_hbm, g1buf, weight_sem.at[4]),
        pltpu.make_async_copy(b3_hbm, b3buf, weight_sem.at[5]),
        pltpu.make_async_copy(w1_hbm, w1buf, weight_sem.at[6]),
        pltpu.make_async_copy(b2_hbm, b2buf, weight_sem.at[7]),
        pltpu.make_async_copy(g2_hbm, g2buf, weight_sem.at[8]),
    ]
    for copy in loads + planes + weights:
        copy.start()

    barrier = pltpu.get_barrier_semaphore()
    for step in range(1, num_dev):
        pl.semaphore_signal(barrier, inc=1, device_id={"seq": peer(step)})

    for copy in loads:
        copy.wait()
    turn = lax.rem(begin - me * feat + window, window)
    plain = pltpu.roll(wbuf[...], turn, 1)[:, 0:feat]
    scale = pltpu.roll(jnp.broadcast_to(modbuf[0], (8, window)), turn, 1)[0:1, 0:feat]
    shift = pltpu.roll(jnp.broadcast_to(modbuf[1], (8, window)), turn, 1)[0:1, 0:feat]
    weight = plain * (1.0 + scale)
    high = weight.astype(BF16)
    low = (weight - high.astype(F32)).astype(BF16)
    stack = jnp.concatenate([high, low], axis=0)
    sums = jnp.sum(high.astype(F32) + low.astype(F32), axis=1, keepdims=True)
    base = jnp.sum(plain * shift, axis=1, keepdims=True)
    both = jnp.concatenate([sums, base], axis=0)
    line = jnp.transpose(jnp.broadcast_to(both, (2 * patch, 8)))

    core = lax.rem(me, 2)
    mine = me // 2
    pairs = num_dev // 2

    def swap(f):
        return [
            pltpu.make_async_remote_copy(
                src_ref=pairstat.at[f, 1 - core], dst_ref=gotpairstat.at[f], send_sem=pair_send.at[f, 0],
                recv_sem=pair_recv.at[f, 0], device_id={"seq": peer(1)}),
            pltpu.make_async_remote_copy(
                src_ref=pair.at[f, 1 - core], dst_ref=gotpair.at[f], send_sem=pair_send.at[f, 1],
                recv_sem=pair_recv.at[f, 1], device_id={"seq": peer(1)}),
        ]

    def transfer(f, other, slot):
        return [
            pltpu.make_async_remote_copy(
                src_ref=stat.at[f, other // 2], dst_ref=gotstat.at[f, slot], send_sem=stat_send.at[f, other // 2],
                recv_sem=stat_recv.at[f, slot], device_id={"seq": other}),
            pltpu.make_async_remote_copy(
                src_ref=send.at[f, other // 2], dst_ref=got.at[f, slot], send_sem=send_sem.at[f, other // 2],
                recv_sem=recv_sem.at[f, slot], device_id={"seq": other}),
        ]

    def messages(f):
        out = []
        for step in range(num_dev - 2, 0, -2):
            out += transfer(f, peer(step), mine)
        return out

    def arrivals(f):
        out = []
        for step in range(num_dev - 2, 0, -2):
            out += transfer(f, peer(step), peer(step) // 2)
        return out

    for f in range(frames):
        planes[f].wait()
        block = xbuf[f]
        full = jnp.dot(stack, block, preferred_element_type=F32)
        values = block.astype(F32)
        mean = jnp.sum(values, axis=0, keepdims=True) * (1.0 / feat)
        centred = values - mean
        spread = jnp.sum(centred * centred, axis=0, keepdims=True)
        part = full[:patch] + full[patch:] - sums * mean
        flat = jnp.transpose(part).reshape(pairs, 2, 2, half, patch)
        for c in range(2):
            pair[f, c] = jnp.concatenate([flat[:, c, 0], flat[:, c, 1]], axis=-1)
            for i in range(pairs):
                at = slice((2 * i + c) * tile, (2 * i + c + 1) * tile)
                pairstat[f, c, i, 0:1, 0:tile] = mean[:, at]
                pairstat[f, c, i, 1:2, 0:tile] = spread[:, at]
                pairstat[f, c, i, 2:3, :] = line[0:1]
                pairstat[f, c, i, 3:8, :] = jnp.zeros((5, 128), F32)
        if f == 0:
            pl.semaphore_wait(barrier, num_dev - 1)
        for copy in swap(f):
            copy.start()
    for f in range(frames):
        for copy in swap(f):
            copy.wait_recv()
        send[f] = (pair[f, core] + gotpair[f]).astype(BF16)
        stat[f, :, 0:3, :] = pairstat[f, core, :, 0:3, :]
        stat[f, :, 3:6, :] = gotpairstat[f, :, 0:3, :]
        for copy in messages(f):
            copy.start()
        got[f, mine] = send[f, mine]
        gotstat[f, mine] = stat[f, mine]

    for copy in weights:
        copy.wait()
    taps = [[jnp.transpose(upbuf[r, c].astype(F32)) for c in range(3)] for r in range(3)]
    for p in range(2):
        for i in range(2):
            group = ((0,), (1, 2)) if p == 0 else ((0, 1), (2,))
            tall = [functools.reduce(lambda a, b: a + b, [taps[r][c] for r in group[i]]) for c in range(3)]
            for q in range(2):
                first = tall[0] if q == 0 else tall[0] + tall[1]
                second = tall[1] + tall[2] if q == 0 else tall[2]
                w2_ref[p, i, q, 0:c1, :] = first.astype(BF16)
                w2_ref[p, i, q, c1 : 2 * c1, :] = second.astype(BF16)
    w3_ref[...] = jnp.zeros(w3_ref.shape, BF16)
    b1_ref[...] = b1buf[...].reshape(1, c1)
    g1_ref[...] = g1buf[...].reshape(1, c1)
    b2_ref[...] = b2buf[...].reshape(1, c2)
    g2_ref[...] = g2buf[...].reshape(1, c2)
    b3 = jnp.concatenate([b3buf[...].reshape(1, c3), jnp.zeros((1, 128 - c3), F32)], axis=1)
    ch = patch // 4
    blank = jnp.zeros((ch, c1), BF16)
    for a in range(2):
        for b in range(3):
            for j in range(4):
                spot = slice((4 * b + j) * ch, (4 * b + j + 1) * ch)
                w1s[a, spot, 0:c1] = w1buf[a + 1, b, j] if j < 3 else blank
                w1s[a, spot, c1 : 2 * c1] = w1buf[a + 1, b, j - 1] if j > 0 else blank
    for b in range(3):
        for e in range(3):
            w3_ref[b, e * 256 : e * 256 + c2, 0:c3] = outbuf[1, b, e]
            w3_ref[b, e * 256 : e * 256 + c2, 128 : 128 + c3] = outbuf[0, b, e]

    def to_next(f):
        return pltpu.make_async_remote_copy(
            src_ref=rows.at[f, 1], dst_ref=rows.at[f, 0], send_sem=halo_send.at[f, 0],
            recv_sem=halo_recv.at[f, 0], device_id={"seq": lax.rem(me + 1, num_dev)})

    def to_last(f):
        return pltpu.make_async_remote_copy(
            src_ref=rows.at[f, 1], dst_ref=rows.at[f, 2], send_sem=halo_send.at[f, 1],
            recv_sem=halo_recv.at[f, 1], device_id={"seq": lax.rem(me + num_dev - 1, num_dev)})

    def merge(f):
        for copy in arrivals(f):
            copy.wait_recv()
        means = jnp.concatenate([gotstat[f, :, 0, :], gotstat[f, :, 3, :]], axis=0)
        off = means - jnp.mean(means, axis=0, keepdims=True)
        spread = jnp.sum(gotstat[f, :, 1, :] + gotstat[f, :, 4, :], axis=0, keepdims=True)
        var = (spread + feat * jnp.sum(off * off, axis=0, keepdims=True)) * (1.0 / width)
        scale = jnp.transpose(jnp.broadcast_to(lax.rsqrt(var + 1e-06), (8, 128)))[0:tile, 0:1]
        lines = jnp.concatenate([gotstat[f, :, 2, :], gotstat[f, :, 5, :]], axis=0)
        fixed = jnp.dot(jnp.transpose(off), lines[:, 0:patch], precision=HIGH, preferred_element_type=F32)[0:tile]
        total_base = jnp.sum(lines, axis=0, keepdims=True)[:, patch:] + biasbuf[...].reshape(1, patch)
        summed = got[f, 0].astype(F32)
        for i in range(1, pairs):
            summed = summed + got[f, i].astype(F32)
        summed = jnp.concatenate([summed[:, :patch], summed[:, patch:]], axis=0)
        done = ((summed + fixed) * scale + total_base).astype(BF16).astype(F32)
        rows[f, 1] = jnp.concatenate([done[:half], done[half:]], axis=1).astype(BF16)

        @pl.when(me < num_dev - 1)
        def _():
            to_next(f).start()

        @pl.when(me > 0)
        def _():
            to_last(f).start()

        @pl.when(me == 0)
        def _():
            rows[f, 0] = jnp.zeros((half, 128), BF16)

        @pl.when(me == num_dev - 1)
        def _():
            rows[f, 2] = jnp.zeros((half, 128), BF16)

    def gather(f):
        @pl.when(me > 0)
        def _():
            to_next(f).wait_recv()

        @pl.when(me < num_dev - 1)
        def _():
            to_last(f).wait_recv()

        quads = []
        col = lax.broadcasted_iota(jnp.int32, (tile, 1), 0)
        for h in range(3):
            pair = rows[f, h].astype(F32)
            token = jnp.concatenate([pair[:, :patch], pair[:, patch:]], axis=0)
            before = jnp.where(col == 0, 0.0, pltpu.roll(token, 1, 0))
            after = jnp.where(col == tile - 1, 0.0, pltpu.roll(token, tile - 1, 0))
            for q in range(2):
                a = 2 * q * ch
                quads.append(jnp.concatenate(
                    [before[:, a + ch : a + 2 * ch], token[:, a : a + 2 * ch], after[:, a : a + ch]], axis=1))
        for i in range(4):
            x1_ref[f, i] = jnp.concatenate(quads[i : i + 3], axis=1).astype(BF16)

    merge(0)
    gather(0)
    stage_in(num_dev, me, 0, x1_ref, w1s, b1_ref, g1_ref, act1)
    stage_up(num_dev, me, act1, w2_ref, b2_ref, g2_ref, act2)
    merge(1)
    m3 = (act2.shape[0] - 2) * TOK_W
    for s in range(4):
        old = stage_out(act2, w3_ref, slice(0, 256), s)
        res_ref[pl.ds(s, m3, stride=4), :] = old[:, 0:128] + b3
        res_ref[pl.ds(4 * m3 + s, m3, stride=4), :] = old[:, 128:256] + b3
    gather(1)

    for f in range(frames):
        for copy in swap(f) + messages(f):
            copy.wait_send()
        @pl.when(me < num_dev - 1)
        def _():
            to_next(f).wait_send()

        @pl.when(me > 0)
        def _():
            to_last(f).wait_send()


def local(
    hidden, mod_shift, mod_scale, head_weight, head_bias, conv_in_weight, conv_in_bias, gain_in,
    up_weight, up_bias, gain_up, out_weight, out_bias,
):
    num_dev = lax.axis_size("seq")
    frames, feat, tok_total = hidden.shape
    tile = tok_total // num_dev
    rows_dev = tile // TOK_W
    patch, width = head_weight.shape
    lat_ch, c1 = conv_in_weight.shape[3:]
    c2, c3 = out_weight.shape[3:]
    lat_rows = 2 * rows_dev
    window = min(width, (feat + 255 - math.gcd(feat, 128)) // 128 * 128)
    vmem = pl.BlockSpec(memory_space=pltpu.VMEM)
    hbm = pl.BlockSpec(memory_space=pltpu.HBM)
    half = tile // 2
    pairs = num_dev // 2
    raw = (hidden, head_weight, mod_scale[None], mod_shift[None], head_bias,
           jnp.transpose(up_weight, (0, 1, 3, 2)), out_weight, conv_in_weight,
           conv_in_bias, gain_in, up_bias, gain_up, out_bias)
    cells = frames * 2 * lat_rows * 4 * TOK_W
    act1 = pltpu.VMEM((lat_rows + 2, TOK_W, 4 * c1), BF16)
    act2 = pltpu.VMEM((2 * lat_rows + 2, TOK_W, 6 * 256), BF16)
    made = pl.pallas_call(
        functools.partial(exchange_kernel, num_dev),
        out_shape=[
            jax.ShapeDtypeStruct((frames, lat_rows + 2, TOK_W, 12 * lat_ch), BF16),
            jax.ShapeDtypeStruct((2, 12 * lat_ch, 2 * c1), BF16),
            jax.ShapeDtypeStruct((2, 2, 2, 2 * c1, c2), BF16),
            jax.ShapeDtypeStruct((3, 768, 256), BF16),
            jax.ShapeDtypeStruct((1, c1), F32),
            jax.ShapeDtypeStruct((1, c1), F32),
            jax.ShapeDtypeStruct((1, c2), F32),
            jax.ShapeDtypeStruct((1, c2), F32),
            jax.ShapeDtypeStruct((cells, 128), F32),
        ],
        in_specs=[hbm] * len(raw),
        out_specs=[vmem] * 9,
        scratch_shapes=[
            pltpu.VMEM((frames, feat, tok_total), BF16),
            pltpu.VMEM((patch, window), F32),
            pltpu.VMEM((2, 1, window), F32),
            pltpu.VMEM((3, 3, c2, c1), BF16),
            pltpu.VMEM((2, 3, 3, c2, c3), BF16),
            pltpu.VMEM((3, 3, 3, lat_ch, c1), BF16),
            pltpu.VMEM((patch,), F32),
            pltpu.VMEM((c1,), F32),
            pltpu.VMEM((c1,), F32),
            pltpu.VMEM((c2,), F32),
            pltpu.VMEM((c2,), F32),
            pltpu.VMEM((c3,), F32),
            act1,
            act2,
            pltpu.VMEM((frames, 2, pairs, half, 2 * patch), F32),
            pltpu.VMEM((frames, 2, pairs, 8, 128), F32),
            pltpu.VMEM((frames, pairs, half, 2 * patch), F32),
            pltpu.VMEM((frames, pairs, 8, 128), F32),
            pltpu.VMEM((frames, pairs, half, 2 * patch), BF16),
            pltpu.VMEM((frames, pairs, 8, 128), F32),
            pltpu.VMEM((frames, pairs, half, 2 * patch), BF16),
            pltpu.VMEM((frames, pairs, 8, 128), F32),
            pltpu.VMEM((frames, 3, half, 2 * patch), BF16),
            pltpu.SemaphoreType.DMA((5,)),
            pltpu.SemaphoreType.DMA((9,)),
            pltpu.SemaphoreType.DMA((frames, 2)),
            pltpu.SemaphoreType.DMA((frames, 2)),
            pltpu.SemaphoreType.DMA((frames, pairs)),
            pltpu.SemaphoreType.DMA((frames, pairs)),
            pltpu.SemaphoreType.DMA((frames, pairs)),
            pltpu.SemaphoreType.DMA((frames, pairs)),
            pltpu.SemaphoreType.DMA((frames, 2)),
            pltpu.SemaphoreType.DMA((frames, 2)),
        ],
        compiler_params=pltpu.CompilerParams(
            vmem_limit_bytes=26 * 1024 * 1024, collective_id=0, has_side_effects=True),
    )(*[pltpu.with_memory_space_constraint(value, pltpu.HBM) for value in raw])
    x1, w1s, w2, w3, b1, g1, b2, g2, res = made
    out = pl.pallas_call(
        functools.partial(conv_kernel, num_dev),
        out_shape=jax.ShapeDtypeStruct((frames * 2 * lat_rows, c3, 4 * TOK_W), BF16),
        in_specs=[vmem] * 9,
        out_specs=hbm,
        scratch_shapes=[
            act1,
            act2,
            pltpu.VMEM((cells // 2, 128), F32),
            pltpu.VMEM((frames * 2 * lat_rows, c3, 4 * TOK_W), BF16),
            pltpu.SemaphoreType.DMA((frames * 2 * lat_rows,)),
        ],
        compiler_params=pltpu.CompilerParams(vmem_limit_bytes=26 * 1024 * 1024),
    )(x1, w1s, b1, g1, w2, b2, g2, w3, res)
    return out.reshape(frames, 2 * lat_rows, c3, 4 * TOK_W).transpose(0, 1, 3, 2)


def solution(mesh):
    placed = (P("grp", "seq", None), P(), P(), P(), P(), P(), P(), P(), P(), P(), P(), P(), P())
    return jax.shard_map(
        local, mesh=mesh, in_specs=placed, out_specs=P("grp", "seq", None, None), check_vma=False
    )
```

```python
import functools
import math

import jax
import jax.numpy as jnp
from jax import lax
from jax.experimental import pallas as pl
from jax.experimental.pallas import tpu as pltpu
from jax.sharding import PartitionSpec as P

TOK_W = 80
HIGH = lax.Precision.HIGHEST
F32 = jnp.float32
BF16 = jnp.bfloat16


def rms_silu(values, gain_vec):
    squares = jnp.mean(values * values, axis=-1, keepdims=True)
    normed = values * lax.rsqrt(squares + 1e-06) * gain_vec
    return normed * jax.nn.sigmoid(normed)


def shift_cols(values, step):
    count = values.shape[0]
    col = lax.broadcasted_iota(jnp.int32, (count, 1), 0) % TOK_W
    if step > 0:
        return jnp.where(col == 0, 0.0, pltpu.roll(values, 1, 0))
    return jnp.where(col == TOK_W - 1, 0.0, pltpu.roll(values, count - 1, 0))


def inside(count, first, step, total):
    row = lax.broadcasted_iota(jnp.int32, (count, 1), 0) // TOK_W * step + first
    return (row >= 0) & (row < total)


def stage_in(num_dev, dev, frame, x_ref, w1s, b1_ref, g1_ref, act1):
    rows1 = x_ref.shape[1]
    lat_rows = rows1 - 2
    c1 = g1_ref.shape[1]
    m1 = rows1 * TOK_W
    keep1 = inside(m1, dev * lat_rows - 1, 1, num_dev * lat_rows)
    x_now = x_ref[frame].reshape(m1, x_ref.shape[-1])
    pre = jnp.dot(x_now, w1s[1], preferred_element_type=F32)
    if frame == 1:
        x_old = x_ref[0].reshape(m1, x_ref.shape[-1])
        pre = pre + jnp.dot(x_old, w1s[0], preferred_element_type=F32)
    for r in range(2):
        val = rms_silu(pre[:, r * c1 : (r + 1) * c1] + b1_ref[...], g1_ref[...])
        val = jnp.where(keep1, val, 0.0)
        edge = shift_cols(val, 1) if r == 1 else shift_cols(val, -1)
        spot = 0 if r == 1 else 3
        act1[:, :, (r + 1) * c1 : (r + 2) * c1] = val.astype(BF16).reshape(rows1, TOK_W, c1)
        act1[:, :, spot * c1 : (spot + 1) * c1] = edge.astype(BF16).reshape(rows1, TOK_W, c1)


def stage_up(num_dev, dev, act1, w2_ref, b2_ref, g2_ref, act2):
    rows2 = act1.shape[0] - 1
    lat_rows = rows2 - 1
    c1 = act1.shape[2] // 4
    c2 = g2_ref.shape[1]
    m2 = rows2 * TOK_W
    start = (0, 1, 1, 2)
    for p in range(2):
        first = 0 if p == 0 else -1
        keep2 = inside(m2, 2 * dev * lat_rows + first, 2, 2 * num_dev * lat_rows)
        for s in range(4):
            q = s % 2
            lanes = slice(start[s] * c1, (start[s] + 2) * c1)
            top = act1[0:rows2, :, lanes].reshape(m2, 2 * c1)
            low = act1[1 : rows2 + 1, :, lanes].reshape(m2, 2 * c1)
            pre = jnp.dot(top, w2_ref[p, 0, q], preferred_element_type=F32)
            pre = pre + jnp.dot(low, w2_ref[p, 1, q], preferred_element_type=F32)
            val = rms_silu(pre + b2_ref[...], g2_ref[...])
            val = jnp.where(keep2, val, 0.0)
            val = jnp.concatenate([val, jnp.zeros((m2, 256 - c2), F32)], axis=1)
            pieces = [(s + 1, val)]
            if s == 3:
                pieces.append((0, shift_cols(val, 1)))
            if s == 0:
                pieces.append((5, shift_cols(val, -1)))
            for spot, piece in pieces:
                piece = piece.astype(BF16).reshape(rows2, TOK_W, 256)
                for i in range(rows2):
                    act2[2 * i + 1 - p, :, spot * 256 : (spot + 1) * 256] = piece[i]


def stage_out(act2, weight, s, cols):
    rows3 = act2.shape[0] - 2
    lanes = slice(s * 256, (s + cols) * 256)
    total = None
    for b in range(3):
        block = act2[b : b + rows3, :, lanes].reshape(rows3 * TOK_W, cols * 256)
        one = jnp.dot(block, weight[b], preferred_element_type=F32)
        total = one if total is None else total + one
    return total


def conv_kernel(num_dev, x_ref, w1s, b1_ref, g1_ref, w2_ref, b2_ref, g2_ref, w3_ref, res_ref, out_hbm,
                act1, act2, res, obuf, out_sem):
    dev = lax.axis_index("seq")
    rows3 = act2.shape[0] - 2
    m3 = rows3 * TOK_W
    c3 = obuf.shape[1]
    width = 4 * TOK_W
    copies = [pltpu.make_async_copy(obuf.at[i], out_hbm.at[i], out_sem.at[i]) for i in range(2 * rows3)]
    stage_in(num_dev, dev, 1, x_ref, w1s, b1_ref, g1_ref, act1)
    for i in range(rows3):
        obuf[i] = jnp.transpose(res_ref[i * width : (i + 1) * width, :])[0:c3].astype(BF16)
        copies[i].start()
    stage_up(num_dev, dev, act1, w2_ref, b2_ref, g2_ref, act2)
    for s in (0, 2):
        new = stage_out(act2, w3_ref, s, 4)
        for g in range(2):
            old = res_ref[pl.ds(4 * m3 + s + g, m3, stride=4), :]
            res[pl.ds(s + g, m3, stride=4), :] = new[:, g * 128 : (g + 1) * 128] + old
    for i in range(rows3):
        obuf[rows3 + i] = jnp.transpose(res[i * width : (i + 1) * width, :])[0:c3].astype(BF16)
        copies[rows3 + i].start()
    for copy in copies:
        copy.wait()


def exchange_kernel(num_dev, x_hbm, w_hbm, scale_hbm, shift_hbm, bias_hbm, up_hbm, outw_hbm, w1_hbm,
                    b1_hbm, g1_hbm, b2_hbm, g2_hbm, b3_hbm,
                    x1_ref, w1s, w2_ref, w3_ref, b1_ref, g1_ref, b2_ref, g2_ref, res_ref,
                    xbuf, wbuf, modbuf, upbuf, outbuf, w1buf, biasbuf, b1buf, g1buf, b2buf, g2buf, b3buf, w3s, act1, act2, pair, pairstat, gotpair, gotpairstat, send, stat, got, gotstat, rows,
                    in_sem, weight_sem, pair_send, pair_recv, send_sem, recv_sem, stat_send, stat_recv, halo_send, halo_recv):
    frames, feat, total = x_hbm.shape
    patch, width = w_hbm.shape
    tile = total // num_dev
    half = tile // 2
    c1, c2 = up_hbm.shape[3], up_hbm.shape[2]
    c3 = outw_hbm.shape[4]
    me = lax.axis_index("seq")

    def peer(step):
        spot = me
        bit = 1
        while bit < num_dev:
            if step & bit:
                spot = spot + (1 - 2 * ((me // bit) % 2)) * bit
            bit *= 2
        return spot

    window = wbuf.shape[1]
    begin = jnp.minimum((me * feat) // 128 * 128, width - window)
    lanes = pl.ds(pl.multiple_of(begin, 128), window)
    loads = [
        pltpu.make_async_copy(w_hbm.at[:, lanes], wbuf, in_sem.at[0]),
        pltpu.make_async_copy(scale_hbm.at[:, lanes], modbuf.at[0], in_sem.at[1]),
        pltpu.make_async_copy(shift_hbm.at[:, lanes], modbuf.at[1], in_sem.at[2]),
    ]
    planes = [pltpu.make_async_copy(x_hbm.at[f], xbuf.at[f], in_sem.at[3 + f]) for f in range(frames)]
    weights = [
        pltpu.make_async_copy(up_hbm, upbuf, weight_sem.at[0]),
        pltpu.make_async_copy(outw_hbm.at[pl.ds(1, 2)], outbuf, weight_sem.at[1]),
        pltpu.make_async_copy(bias_hbm, biasbuf, weight_sem.at[2]),
        pltpu.make_async_copy(b1_hbm, b1buf, weight_sem.at[3]),
        pltpu.make_async_copy(g1_hbm, g1buf, weight_sem.at[4]),
        pltpu.make_async_copy(b3_hbm, b3buf, weight_sem.at[5]),
        pltpu.make_async_copy(w1_hbm, w1buf, weight_sem.at[6]),
        pltpu.make_async_copy(b2_hbm, b2buf, weight_sem.at[7]),
        pltpu.make_async_copy(g2_hbm, g2buf, weight_sem.at[8]),
    ]
    for copy in loads + planes + weights:
        copy.start()

    barrier = pltpu.get_barrier_semaphore()
    for step in range(1, num_dev):
        pl.semaphore_signal(barrier, inc=1, device_id={"seq": peer(step)})

    for copy in loads:
        copy.wait()
    turn = lax.rem(begin - me * feat + window, window)
    plain = pltpu.roll(wbuf[...], turn, 1)[:, 0:feat]
    scale = pltpu.roll(jnp.broadcast_to(modbuf[0], (8, window)), turn, 1)[0:1, 0:feat]
    shift = pltpu.roll(jnp.broadcast_to(modbuf[1], (8, window)), turn, 1)[0:1, 0:feat]
    weight = plain * (1.0 + scale)
    high = weight.astype(BF16)
    low = (weight - high.astype(F32)).astype(BF16)
    stack = jnp.concatenate([high, low], axis=0)
    sums = jnp.sum(high.astype(F32) + low.astype(F32), axis=1, keepdims=True)
    base = jnp.sum(plain * shift, axis=1, keepdims=True)
    both = jnp.concatenate([sums, base], axis=0)
    line = jnp.transpose(jnp.broadcast_to(both, (2 * patch, 8)))

    core = lax.rem(me, 2)
    mine = me // 2
    pairs = num_dev // 2

    def swap(f):
        return [
            pltpu.make_async_remote_copy(
                src_ref=pairstat.at[f, 1 - core], dst_ref=gotpairstat.at[f], send_sem=pair_send.at[f, 0],
                recv_sem=pair_recv.at[f, 0], device_id={"seq": peer(1)}),
            pltpu.make_async_remote_copy(
                src_ref=pair.at[f, 1 - core], dst_ref=gotpair.at[f], send_sem=pair_send.at[f, 1],
                recv_sem=pair_recv.at[f, 1], device_id={"seq": peer(1)}),
        ]

    def transfer(f, other, slot):
        return [
            pltpu.make_async_remote_copy(
                src_ref=stat.at[f, other // 2], dst_ref=gotstat.at[f, slot], send_sem=stat_send.at[f, other // 2],
                recv_sem=stat_recv.at[f, slot], device_id={"seq": other}),
            pltpu.make_async_remote_copy(
                src_ref=send.at[f, other // 2], dst_ref=got.at[f, slot], send_sem=send_sem.at[f, other // 2],
                recv_sem=recv_sem.at[f, slot], device_id={"seq": other}),
        ]

    def messages(f):
        out = []
        for step in range(num_dev - 2, 0, -2):
            out += transfer(f, peer(step), mine)
        return out

    def arrivals(f):
        out = []
        for step in range(num_dev - 2, 0, -2):
            out += transfer(f, peer(step), peer(step) // 2)
        return out

    for f in range(frames):
        planes[f].wait()
        block = xbuf[f]
        full = jnp.dot(stack, block, preferred_element_type=F32)
        values = block.astype(F32)
        mean = jnp.sum(values, axis=0, keepdims=True) * (1.0 / feat)
        centred = values - mean
        spread = jnp.sum(centred * centred, axis=0, keepdims=True)
        part = full[:patch] + full[patch:] - sums * mean
        flat = jnp.transpose(part).reshape(pairs, 2, 2, half, patch)
        for c in range(2):
            pair[f, c] = jnp.concatenate([flat[:, c, 0], flat[:, c, 1]], axis=-1)
            for i in range(pairs):
                at = slice((2 * i + c) * tile, (2 * i + c + 1) * tile)
                pairstat[f, c, i, 0:1, 0:tile] = mean[:, at]
                pairstat[f, c, i, 1:2, 0:tile] = spread[:, at]
                pairstat[f, c, i, 2:3, :] = line[0:1]
                pairstat[f, c, i, 3:8, :] = jnp.zeros((5, 128), F32)
        if f == 0:
            pl.semaphore_wait(barrier, num_dev - 1)
        for copy in swap(f):
            copy.start()
    for f in range(frames):
        for copy in swap(f):
            copy.wait_recv()
        send[f] = (pair[f, core] + gotpair[f]).astype(BF16)
        stat[f, :, 0:3, :] = pairstat[f, core, :, 0:3, :]
        stat[f, :, 3:6, :] = gotpairstat[f, :, 0:3, :]
        for copy in messages(f):
            copy.start()
        got[f, mine] = send[f, mine]
        gotstat[f, mine] = stat[f, mine]

    for copy in weights:
        copy.wait()
    taps = [[jnp.transpose(upbuf[r, c].astype(F32)) for c in range(3)] for r in range(3)]
    for p in range(2):
        for i in range(2):
            group = ((0,), (1, 2)) if p == 0 else ((0, 1), (2,))
            tall = [functools.reduce(lambda a, b: a + b, [taps[r][c] for r in group[i]]) for c in range(3)]
            for q in range(2):
                first = tall[0] if q == 0 else tall[0] + tall[1]
                second = tall[1] + tall[2] if q == 0 else tall[2]
                w2_ref[p, i, q, 0:c1, :] = first.astype(BF16)
                w2_ref[p, i, q, c1 : 2 * c1, :] = second.astype(BF16)
    w3s[...] = jnp.zeros(w3s.shape, BF16)
    w3_ref[...] = jnp.zeros(w3_ref.shape, BF16)
    b1_ref[...] = b1buf[...].reshape(1, c1)
    g1_ref[...] = g1buf[...].reshape(1, c1)
    b2_ref[...] = b2buf[...].reshape(1, c2)
    g2_ref[...] = g2buf[...].reshape(1, c2)
    b3 = jnp.concatenate([b3buf[...].reshape(1, c3), jnp.zeros((1, 128 - c3), F32)], axis=1)
    ch = patch // 4
    blank = jnp.zeros((ch, c1), BF16)
    for a in range(2):
        for b in range(3):
            for j in range(4):
                spot = slice((4 * b + j) * ch, (4 * b + j + 1) * ch)
                w1s[a, spot, 0:c1] = w1buf[a + 1, b, j] if j < 3 else blank
                w1s[a, spot, c1 : 2 * c1] = w1buf[a + 1, b, j - 1] if j > 0 else blank
    for b in range(3):
        for e in range(3):
            w3s[b, e * 256 : e * 256 + c2, 0:c3] = outbuf[1, b, e]
            w3s[b, e * 256 : e * 256 + c2, 128 : 128 + c3] = outbuf[0, b, e]
            for g in range(2):
                w3_ref[b, (e + g) * 256 : (e + g) * 256 + c2, g * 128 : g * 128 + c3] = outbuf[1, b, e]

    def to_next(f):
        return pltpu.make_async_remote_copy(
            src_ref=rows.at[f, 1], dst_ref=rows.at[f, 0], send_sem=halo_send.at[f, 0],
            recv_sem=halo_recv.at[f, 0], device_id={"seq": lax.rem(me + 1, num_dev)})

    def to_last(f):
        return pltpu.make_async_remote_copy(
            src_ref=rows.at[f, 1], dst_ref=rows.at[f, 2], send_sem=halo_send.at[f, 1],
            recv_sem=halo_recv.at[f, 1], device_id={"seq": lax.rem(me + num_dev - 1, num_dev)})

    def merge(f):
        for copy in arrivals(f):
            copy.wait_recv()
        means = jnp.concatenate([gotstat[f, :, 0, :], gotstat[f, :, 3, :]], axis=0)
        off = means - jnp.mean(means, axis=0, keepdims=True)
        spread = jnp.sum(gotstat[f, :, 1, :] + gotstat[f, :, 4, :], axis=0, keepdims=True)
        var = (spread + feat * jnp.sum(off * off, axis=0, keepdims=True)) * (1.0 / width)
        scale = jnp.transpose(jnp.broadcast_to(lax.rsqrt(var + 1e-06), (8, 128)))[0:tile, 0:1]
        lines = jnp.concatenate([gotstat[f, :, 2, :], gotstat[f, :, 5, :]], axis=0)
        fixed = jnp.dot(jnp.transpose(off), lines[:, 0:patch], precision=HIGH, preferred_element_type=F32)[0:tile]
        total_base = jnp.sum(lines, axis=0, keepdims=True)[:, patch:] + biasbuf[...].reshape(1, patch)
        summed = got[f, 0].astype(F32)
        for i in range(1, pairs):
            summed = summed + got[f, i].astype(F32)
        summed = jnp.concatenate([summed[:, :patch], summed[:, patch:]], axis=0)
        done = ((summed + fixed) * scale + total_base).astype(BF16).astype(F32)
        rows[f, 1] = jnp.concatenate([done[:half], done[half:]], axis=1).astype(BF16)

        @pl.when(me < num_dev - 1)
        def _():
            to_next(f).start()

        @pl.when(me > 0)
        def _():
            to_last(f).start()

        @pl.when(me == 0)
        def _():
            rows[f, 0] = jnp.zeros((half, 128), BF16)

        @pl.when(me == num_dev - 1)
        def _():
            rows[f, 2] = jnp.zeros((half, 128), BF16)

    def gather(f):
        @pl.when(me > 0)
        def _():
            to_next(f).wait_recv()

        @pl.when(me < num_dev - 1)
        def _():
            to_last(f).wait_recv()

        quads = []
        col = lax.broadcasted_iota(jnp.int32, (tile, 1), 0)
        for h in range(3):
            pair = rows[f, h].astype(F32)
            token = jnp.concatenate([pair[:, :patch], pair[:, patch:]], axis=0)
            before = jnp.where(col == 0, 0.0, pltpu.roll(token, 1, 0))
            after = jnp.where(col == tile - 1, 0.0, pltpu.roll(token, tile - 1, 0))
            for q in range(2):
                a = 2 * q * ch
                quads.append(jnp.concatenate(
                    [before[:, a + ch : a + 2 * ch], token[:, a : a + 2 * ch], after[:, a : a + ch]], axis=1))
        for i in range(4):
            x1_ref[f, i] = jnp.concatenate(quads[i : i + 3], axis=1).astype(BF16)

    merge(0)
    gather(0)
    stage_in(num_dev, me, 0, x1_ref, w1s, b1_ref, g1_ref, act1)
    stage_up(num_dev, me, act1, w2_ref, b2_ref, g2_ref, act2)
    merge(1)
    m3 = (act2.shape[0] - 2) * TOK_W
    for s in range(4):
        old = stage_out(act2, w3s, s, 3)
        res_ref[pl.ds(s, m3, stride=4), :] = old[:, 0:128] + b3
        res_ref[pl.ds(4 * m3 + s, m3, stride=4), :] = old[:, 128:256] + b3
    gather(1)

    for f in range(frames):
        for copy in swap(f) + messages(f):
            copy.wait_send()
        @pl.when(me < num_dev - 1)
        def _():
            to_next(f).wait_send()

        @pl.when(me > 0)
        def _():
            to_last(f).wait_send()


def local(
    hidden, mod_shift, mod_scale, head_weight, head_bias, conv_in_weight, conv_in_bias, gain_in,
    up_weight, up_bias, gain_up, out_weight, out_bias,
):
    num_dev = lax.axis_size("seq")
    frames, feat, tok_total = hidden.shape
    tile = tok_total // num_dev
    rows_dev = tile // TOK_W
    patch, width = head_weight.shape
    lat_ch, c1 = conv_in_weight.shape[3:]
    c2, c3 = out_weight.shape[3:]
    lat_rows = 2 * rows_dev
    window = min(width, (feat + 255 - math.gcd(feat, 128)) // 128 * 128)
    vmem = pl.BlockSpec(memory_space=pltpu.VMEM)
    hbm = pl.BlockSpec(memory_space=pltpu.HBM)
    half = tile // 2
    pairs = num_dev // 2
    raw = (hidden, head_weight, mod_scale[None], mod_shift[None], head_bias,
           jnp.transpose(up_weight, (0, 1, 3, 2)), out_weight, conv_in_weight,
           conv_in_bias, gain_in, up_bias, gain_up, out_bias)
    cells = frames * 2 * lat_rows * 4 * TOK_W
    act1 = pltpu.VMEM((lat_rows + 2, TOK_W, 4 * c1), BF16)
    act2 = pltpu.VMEM((2 * lat_rows + 2, TOK_W, 6 * 256), BF16)
    made = pl.pallas_call(
        functools.partial(exchange_kernel, num_dev),
        out_shape=[
            jax.ShapeDtypeStruct((frames, lat_rows + 2, TOK_W, 12 * lat_ch), BF16),
            jax.ShapeDtypeStruct((2, 12 * lat_ch, 2 * c1), BF16),
            jax.ShapeDtypeStruct((2, 2, 2, 2 * c1, c2), BF16),
            jax.ShapeDtypeStruct((3, 1024, 256), BF16),
            jax.ShapeDtypeStruct((1, c1), F32),
            jax.ShapeDtypeStruct((1, c1), F32),
            jax.ShapeDtypeStruct((1, c2), F32),
            jax.ShapeDtypeStruct((1, c2), F32),
            jax.ShapeDtypeStruct((cells, 128), F32),
        ],
        in_specs=[hbm] * len(raw),
        out_specs=[vmem] * 9,
        scratch_shapes=[
            pltpu.VMEM((frames, feat, tok_total), BF16),
            pltpu.VMEM((patch, window), F32),
            pltpu.VMEM((2, 1, window), F32),
            pltpu.VMEM((3, 3, c2, c1), BF16),
            pltpu.VMEM((2, 3, 3, c2, c3), BF16),
            pltpu.VMEM((3, 3, 3, lat_ch, c1), BF16),
            pltpu.VMEM((patch,), F32),
            pltpu.VMEM((c1,), F32),
            pltpu.VMEM((c1,), F32),
            pltpu.VMEM((c2,), F32),
            pltpu.VMEM((c2,), F32),
            pltpu.VMEM((c3,), F32),
            pltpu.VMEM((3, 768, 256), BF16),
            act1,
            act2,
            pltpu.VMEM((frames, 2, pairs, half, 2 * patch), F32),
            pltpu.VMEM((frames, 2, pairs, 8, 128), F32),
            pltpu.VMEM((frames, pairs, half, 2 * patch), F32),
            pltpu.VMEM((frames, pairs, 8, 128), F32),
            pltpu.VMEM((frames, pairs, half, 2 * patch), BF16),
            pltpu.VMEM((frames, pairs, 8, 128), F32),
            pltpu.VMEM((frames, pairs, half, 2 * patch), BF16),
            pltpu.VMEM((frames, pairs, 8, 128), F32),
            pltpu.VMEM((frames, 3, half, 2 * patch), BF16),
            pltpu.SemaphoreType.DMA((5,)),
            pltpu.SemaphoreType.DMA((9,)),
            pltpu.SemaphoreType.DMA((frames, 2)),
            pltpu.SemaphoreType.DMA((frames, 2)),
            pltpu.SemaphoreType.DMA((frames, pairs)),
            pltpu.SemaphoreType.DMA((frames, pairs)),
            pltpu.SemaphoreType.DMA((frames, pairs)),
            pltpu.SemaphoreType.DMA((frames, pairs)),
            pltpu.SemaphoreType.DMA((frames, 2)),
            pltpu.SemaphoreType.DMA((frames, 2)),
        ],
        compiler_params=pltpu.CompilerParams(
            vmem_limit_bytes=26 * 1024 * 1024, collective_id=0, has_side_effects=True),
    )(*[pltpu.with_memory_space_constraint(value, pltpu.HBM) for value in raw])
    x1, w1s, w2, w3, b1, g1, b2, g2, res = made
    out = pl.pallas_call(
        functools.partial(conv_kernel, num_dev),
        out_shape=jax.ShapeDtypeStruct((frames * 2 * lat_rows, c3, 4 * TOK_W), BF16),
        in_specs=[vmem] * 9,
        out_specs=hbm,
        scratch_shapes=[
            act1,
            act2,
            pltpu.VMEM((cells // 2, 128), F32),
            pltpu.VMEM((frames * 2 * lat_rows, c3, 4 * TOK_W), BF16),
            pltpu.SemaphoreType.DMA((frames * 2 * lat_rows,)),
        ],
        compiler_params=pltpu.CompilerParams(vmem_limit_bytes=26 * 1024 * 1024),
    )(x1, w1s, b1, g1, w2, b2, g2, w3, res)
    return out.reshape(frames, 2 * lat_rows, c3, 4 * TOK_W).transpose(0, 1, 3, 2)


def solution(mesh):
    placed = (P("grp", "seq", None), P(), P(), P(), P(), P(), P(), P(), P(), P(), P(), P(), P())
    return jax.shard_map(
        local, mesh=mesh, in_specs=placed, out_specs=P("grp", "seq", None, None), check_vma=False
    )
```

```python
import functools
import math

import jax
import jax.numpy as jnp
from jax import lax
from jax.experimental import pallas as pl
from jax.experimental.pallas import tpu as pltpu
from jax.sharding import PartitionSpec as P

TOK_W = 80
HIGH = lax.Precision.HIGHEST
F32 = jnp.float32
BF16 = jnp.bfloat16


def rms_silu(values, gain_vec):
    squares = jnp.mean(values * values, axis=-1, keepdims=True)
    normed = values * lax.rsqrt(squares + 1e-06) * gain_vec
    return normed * jax.nn.sigmoid(normed)


def shift_cols(values, step):
    count = values.shape[0]
    col = lax.broadcasted_iota(jnp.int32, (count, 1), 0) % TOK_W
    if step > 0:
        return jnp.where(col == 0, 0.0, pltpu.roll(values, 1, 0))
    return jnp.where(col == TOK_W - 1, 0.0, pltpu.roll(values, count - 1, 0))


def inside(count, first, step, total):
    row = lax.broadcasted_iota(jnp.int32, (count, 1), 0) // TOK_W * step + first
    return (row >= 0) & (row < total)


def stage_in(num_dev, dev, frame, x_ref, w1s, b1_ref, g1_ref, act1, edge1):
    rows1 = x_ref.shape[1]
    lat_rows = rows1 - 2
    c1 = g1_ref.shape[1]
    m1 = rows1 * TOK_W
    keep1 = inside(m1, dev * lat_rows - 1, 1, num_dev * lat_rows)
    x_now = x_ref[frame].reshape(m1, x_ref.shape[-1])
    pre = jnp.dot(x_now, w1s[1], preferred_element_type=F32)
    if frame == 1:
        x_old = x_ref[0].reshape(m1, x_ref.shape[-1])
        pre = pre + jnp.dot(x_old, w1s[0], preferred_element_type=F32)
    for r in range(2):
        val = rms_silu(pre[:, r * c1 : (r + 1) * c1] + b1_ref[...], g1_ref[...])
        val = jnp.where(keep1, val, 0.0)
        act1[:, :, r * c1 : (r + 1) * c1] = val.astype(BF16).reshape(rows1, TOK_W, c1)
        if r == 0:
            moved = shift_cols(val, -1)
            act1[:, :, 2 * c1 : 3 * c1] = moved.astype(BF16).reshape(rows1, TOK_W, c1)
            firsts = [val[i * TOK_W : i * TOK_W + 1] for i in range(rows1)]
            fill = [jnp.zeros((17 - rows1, c1), F32)]
            for k in range(2):
                edge1[k, :, 0:c1] = jnp.zeros((16, c1), BF16)
                edge1[k, :, c1 : 2 * c1] = jnp.concatenate(firsts[k : k + rows1 - 1] + fill, axis=0).astype(BF16)


def silu(values):
    return values * jax.nn.sigmoid(values)


def stage_up(num_dev, dev, act1, edge1, w2_ref, b2_ref, g2_ref, chans, act2):
    rows2 = act1.shape[0] - 1
    lat_rows = rows2 - 1
    c1 = act1.shape[2] // 3
    m2 = rows2 * TOK_W
    left = lax.broadcasted_iota(jnp.int32, (1, 128), 1) < chans - 128
    for t in range(2):
        lanes = slice(t * c1, (t + 2) * c1)
        top = act1[0:rows2, :, lanes].reshape(m2, 2 * c1)
        low = act1[1 : rows2 + 1, :, lanes].reshape(m2, 2 * c1)
        if t == 1:
            top = jnp.concatenate([top, edge1[0]], axis=0)
            low = jnp.concatenate([low, edge1[1]], axis=0)
        count = top.shape[0]
        pre = jnp.dot(top, w2_ref[0], preferred_element_type=F32)
        pre = pre + jnp.dot(low, w2_ref[1], preferred_element_type=F32)
        index = lax.broadcasted_iota(jnp.int32, (count, 1), 0)
        row = jnp.where(index < m2, index // TOK_W, index - m2)
        for p in range(2):
            a = pre[:, p * 384 : p * 384 + 128] + b2_ref[:, 0:128]
            b = pre[:, p * 384 + 128 : p * 384 + 256] + b2_ref[:, 0:128]
            h = pre[:, p * 384 + 256 : p * 384 + 384] + b2_ref[:, 128:256]
            sq = h * h
            sum_a = jnp.sum(a * a + jnp.where(left, sq, 0.0), axis=-1, keepdims=True)
            sum_b = jnp.sum(b * b + jnp.where(left, 0.0, sq), axis=-1, keepdims=True)
            inv_a = lax.rsqrt(sum_a * (1.0 / chans) + 1e-06)
            inv_b = lax.rsqrt(sum_b * (1.0 / chans) + 1e-06)
            line = 2 * dev * lat_rows + 2 * row - p
            keep = (line >= 0) & (line < 2 * num_dev * lat_rows)
            keep_a, keep_b = keep, keep
            if t == 1:
                keep_a = keep & (index < m2)
                keep_b = keep & ((index >= m2) | (index % TOK_W != TOK_W - 1))
            gain_a = jnp.where(keep_a, inv_a, 0.0)
            gain_b = jnp.where(keep_b, inv_b, 0.0)
            a = silu(a * gain_a * g2_ref[:, 0:128])
            b = silu(b * gain_b * g2_ref[:, 0:128])
            h = silu(h * jnp.where(left, gain_a, gain_b) * g2_ref[:, 128:256])
            val = jnp.concatenate([a, b, h], axis=1)
            main = val[0:m2]
            piece = main.astype(BF16).reshape(rows2, TOK_W, 384)
            for i in range(rows2):
                act2[2 * i + 1 - p, :, (t + 1) * 384 : (t + 2) * 384] = piece[i]
            if t == 1:
                moved = pltpu.roll(main, 1, 0)
                col = lax.broadcasted_iota(jnp.int32, (TOK_W, 1), 0)
                for i in range(rows2):
                    block = jnp.where(col == 0, val[m2 + i : m2 + i + 1], moved[i * TOK_W : (i + 1) * TOK_W])
                    act2[2 * i + 1 - p, :, 0:384] = block.astype(BF16)


def stage_out(act2, w3_ref, part, t):
    rows3 = act2.shape[0] - 2
    total = None
    for b in range(3):
        block = act2[b : b + rows3, :, t * 384 : t * 384 + 768].reshape(rows3 * TOK_W, 768)
        one = jnp.dot(block, w3_ref[part, b], preferred_element_type=F32)
        total = one if total is None else total + one
    return total


def conv_kernel(num_dev, chans, x_ref, w1s, b1_ref, g1_ref, w2_ref, b2_ref, g2_ref, w3_ref, res_ref, out_hbm,
                act1, edge1, act2, res, obuf, out_sem):
    dev = lax.axis_index("seq")
    rows3 = act2.shape[0] - 2
    m3 = rows3 * TOK_W
    c3 = obuf.shape[1]
    width = 4 * TOK_W
    copies = [pltpu.make_async_copy(obuf.at[i], out_hbm.at[i], out_sem.at[i]) for i in range(2 * rows3)]
    stage_in(num_dev, dev, 1, x_ref, w1s, b1_ref, g1_ref, act1, edge1)
    for i in range(rows3):
        obuf[i] = jnp.transpose(res_ref[i * width : (i + 1) * width, :])[0:c3].astype(BF16)
        copies[i].start()
    stage_up(num_dev, dev, act1, edge1, w2_ref, b2_ref, g2_ref, chans, act2)
    for s in (0, 2):
        new = stage_out(act2, w3_ref, 0, s // 2)
        for g in range(2):
            old = res_ref[pl.ds(4 * m3 + s + g, m3, stride=4), :]
            res[pl.ds(s + g, m3, stride=4), :] = new[:, g * 128 : (g + 1) * 128] + old
    for i in range(rows3):
        obuf[rows3 + i] = jnp.transpose(res[i * width : (i + 1) * width, :])[0:c3].astype(BF16)
        copies[rows3 + i].start()
    for copy in copies:
        copy.wait()


def exchange_kernel(num_dev, x_hbm, w_hbm, scale_hbm, shift_hbm, bias_hbm, up_hbm, outw_hbm, w1_hbm,
                    b1_hbm, g1_hbm, b2_hbm, g2_hbm, b3_hbm,
                    x1_ref, w1s, w2_ref, w3_ref, b1_ref, g1_ref, b2_ref, g2_ref, res_ref,
                    xbuf, wbuf, modbuf, upbuf, outbuf, w1buf, biasbuf, b1buf, g1buf, b2buf, g2buf, b3buf, act1, edge1, act2, pair, pairstat, gotpair, gotpairstat, send, stat, got, gotstat, rows,
                    in_sem, weight_sem, pair_send, pair_recv, send_sem, recv_sem, stat_send, stat_recv, halo_send, halo_recv):
    frames, feat, total = x_hbm.shape
    patch, width = w_hbm.shape
    tile = total // num_dev
    half = tile // 2
    c1, c2 = up_hbm.shape[3], up_hbm.shape[2]
    c3 = outw_hbm.shape[4]
    me = lax.axis_index("seq")

    def peer(step):
        spot = me
        bit = 1
        while bit < num_dev:
            if step & bit:
                spot = spot + (1 - 2 * ((me // bit) % 2)) * bit
            bit *= 2
        return spot

    window = wbuf.shape[1]
    begin = jnp.minimum((me * feat) // 128 * 128, width - window)
    lanes = pl.ds(pl.multiple_of(begin, 128), window)
    loads = [
        pltpu.make_async_copy(w_hbm.at[:, lanes], wbuf, in_sem.at[0]),
        pltpu.make_async_copy(scale_hbm.at[:, lanes], modbuf.at[0], in_sem.at[1]),
        pltpu.make_async_copy(shift_hbm.at[:, lanes], modbuf.at[1], in_sem.at[2]),
    ]
    planes = [pltpu.make_async_copy(x_hbm.at[f], xbuf.at[f], in_sem.at[3 + f]) for f in range(frames)]
    weights = [
        pltpu.make_async_copy(up_hbm, upbuf, weight_sem.at[0]),
        pltpu.make_async_copy(outw_hbm.at[pl.ds(1, 2)], outbuf, weight_sem.at[1]),
        pltpu.make_async_copy(bias_hbm, biasbuf, weight_sem.at[2]),
        pltpu.make_async_copy(b1_hbm, b1buf, weight_sem.at[3]),
        pltpu.make_async_copy(g1_hbm, g1buf, weight_sem.at[4]),
        pltpu.make_async_copy(b3_hbm, b3buf, weight_sem.at[5]),
        pltpu.make_async_copy(w1_hbm, w1buf, weight_sem.at[6]),
        pltpu.make_async_copy(b2_hbm, b2buf, weight_sem.at[7]),
        pltpu.make_async_copy(g2_hbm, g2buf, weight_sem.at[8]),
    ]
    for copy in loads + planes + weights:
        copy.start()

    barrier = pltpu.get_barrier_semaphore()
    for step in range(1, num_dev):
        pl.semaphore_signal(barrier, inc=1, device_id={"seq": peer(step)})

    for copy in loads:
        copy.wait()
    turn = lax.rem(begin - me * feat + window, window)
    plain = pltpu.roll(wbuf[...], turn, 1)[:, 0:feat]
    scale = pltpu.roll(jnp.broadcast_to(modbuf[0], (8, window)), turn, 1)[0:1, 0:feat]
    shift = pltpu.roll(jnp.broadcast_to(modbuf[1], (8, window)), turn, 1)[0:1, 0:feat]
    weight = plain * (1.0 + scale)
    high = weight.astype(BF16)
    low = (weight - high.astype(F32)).astype(BF16)
    stack = jnp.concatenate([high, low], axis=0)
    sums = jnp.sum(high.astype(F32) + low.astype(F32), axis=1, keepdims=True)
    base = jnp.sum(plain * shift, axis=1, keepdims=True)
    both = jnp.concatenate([sums, base], axis=0)
    line = jnp.transpose(jnp.broadcast_to(both, (2 * patch, 8)))

    core = lax.rem(me, 2)
    mine = me // 2
    pairs = num_dev // 2

    def swap(f):
        return [
            pltpu.make_async_remote_copy(
                src_ref=pairstat.at[f, 1 - core], dst_ref=gotpairstat.at[f], send_sem=pair_send.at[f, 0],
                recv_sem=pair_recv.at[f, 0], device_id={"seq": peer(1)}),
            pltpu.make_async_remote_copy(
                src_ref=pair.at[f, 1 - core], dst_ref=gotpair.at[f], send_sem=pair_send.at[f, 1],
                recv_sem=pair_recv.at[f, 1], device_id={"seq": peer(1)}),
        ]

    def transfer(f, other, slot):
        return [
            pltpu.make_async_remote_copy(
                src_ref=stat.at[f, other // 2], dst_ref=gotstat.at[f, slot], send_sem=stat_send.at[f, other // 2],
                recv_sem=stat_recv.at[f, slot], device_id={"seq": other}),
            pltpu.make_async_remote_copy(
                src_ref=send.at[f, other // 2], dst_ref=got.at[f, slot], send_sem=send_sem.at[f, other // 2],
                recv_sem=recv_sem.at[f, slot], device_id={"seq": other}),
        ]

    def messages(f):
        out = []
        for step in range(num_dev - 2, 0, -2):
            out += transfer(f, peer(step), mine)
        return out

    def arrivals(f):
        out = []
        for step in range(num_dev - 2, 0, -2):
            out += transfer(f, peer(step), peer(step) // 2)
        return out

    for f in range(frames):
        planes[f].wait()
        block = xbuf[f]
        full = jnp.dot(stack, block, preferred_element_type=F32)
        values = block.astype(F32)
        mean = jnp.sum(values, axis=0, keepdims=True) * (1.0 / feat)
        centred = values - mean
        spread = jnp.sum(centred * centred, axis=0, keepdims=True)
        part = full[:patch] + full[patch:] - sums * mean
        flat = jnp.transpose(part).reshape(pairs, 2, 2, half, patch)
        for c in range(2):
            pair[f, c] = jnp.concatenate([flat[:, c, 0], flat[:, c, 1]], axis=-1)
            for i in range(pairs):
                at = slice((2 * i + c) * tile, (2 * i + c + 1) * tile)
                pairstat[f, c, i, 0:1, 0:tile] = mean[:, at]
                pairstat[f, c, i, 1:2, 0:tile] = spread[:, at]
                pairstat[f, c, i, 2:3, :] = line[0:1]
                pairstat[f, c, i, 3:8, :] = jnp.zeros((5, 128), F32)
        if f == 0:
            pl.semaphore_wait(barrier, num_dev - 1)
        for copy in swap(f):
            copy.start()
    for f in range(frames):
        for copy in swap(f):
            copy.wait_recv()
        send[f] = (pair[f, core] + gotpair[f]).astype(BF16)
        stat[f, :, 0:3, :] = pairstat[f, core, :, 0:3, :]
        stat[f, :, 3:6, :] = gotpairstat[f, :, 0:3, :]
        for copy in messages(f):
            copy.start()
        got[f, mine] = send[f, mine]
        gotstat[f, mine] = stat[f, mine]

    for copy in weights:
        copy.wait()
    taps = [[jnp.transpose(upbuf[r, c].astype(F32)) for c in range(3)] for r in range(3)]
    for p in range(2):
        for i in range(2):
            group = ((0,), (1, 2)) if p == 0 else ((0, 1), (2,))
            tall = [functools.reduce(lambda a, b: a + b, [taps[r][c] for r in group[i]]) for c in range(3)]
            for q in range(2):
                first = tall[0] if q == 0 else tall[0] + tall[1]
                second = tall[1] + tall[2] if q == 0 else tall[2]
                for k, half_w in enumerate((first, second)):
                    down = slice(k * c1, (k + 1) * c1)
                    lo = p * 384 + (1 - q) * 128
                    hi = p * 384 + 256 + (1 - q) * (c2 - 128)
                    w2_ref[i, down, lo : lo + 128] = half_w[:, 0:128].astype(BF16)
                    w2_ref[i, down, hi : hi + c2 - 128] = half_w[:, 128:c2].astype(BF16)
    w3_ref[...] = jnp.zeros(w3_ref.shape, BF16)
    b1_ref[...] = b1buf[...].reshape(1, c1)
    g1_ref[...] = g1buf[...].reshape(1, c1)
    b2 = b2buf[...].reshape(1, c2)
    g2 = g2buf[...].reshape(1, c2)
    b2_ref[...] = jnp.concatenate([b2, b2[:, 128:c2]], axis=1)
    g2_ref[...] = jnp.concatenate([g2, g2[:, 128:c2]], axis=1)
    b3 = jnp.concatenate([b3buf[...].reshape(1, c3), jnp.zeros((1, 128 - c3), F32)], axis=1)
    ch = patch // 4
    blank = jnp.zeros((ch, c1), BF16)
    for a in range(2):
        for b in range(3):
            for j in range(4):
                spot = slice((4 * b + j) * ch, (4 * b + j + 1) * ch)
                w1s[a, spot, 0:c1] = w1buf[a + 1, b, j] if j < 3 else blank
                w1s[a, spot, c1 : 2 * c1] = w1buf[a + 1, b, j - 1] if j > 0 else blank
    for b in range(3):
        for e in range(3):
            for a in range(2):
                for g in range(2):
                    k = e + g
                    lo = k // 2 * 384 + k % 2 * 128
                    hi = k // 2 * 384 + 256 + k % 2 * (c2 - 128)
                    w3_ref[a, b, lo : lo + 128, g * 128 : g * 128 + c3] = outbuf[1 - a, b, e, 0:128, :]
                    w3_ref[a, b, hi : hi + c2 - 128, g * 128 : g * 128 + c3] = outbuf[1 - a, b, e, 128:c2, :]

    def to_next(f):
        return pltpu.make_async_remote_copy(
            src_ref=rows.at[f, 1], dst_ref=rows.at[f, 0], send_sem=halo_send.at[f, 0],
            recv_sem=halo_recv.at[f, 0], device_id={"seq": lax.rem(me + 1, num_dev)})

    def to_last(f):
        return pltpu.make_async_remote_copy(
            src_ref=rows.at[f, 1], dst_ref=rows.at[f, 2], send_sem=halo_send.at[f, 1],
            recv_sem=halo_recv.at[f, 1], device_id={"seq": lax.rem(me + num_dev - 1, num_dev)})

    def merge(f):
        for copy in arrivals(f):
            copy.wait_recv()
        means = jnp.concatenate([gotstat[f, :, 0, :], gotstat[f, :, 3, :]], axis=0)
        off = means - jnp.mean(means, axis=0, keepdims=True)
        spread = jnp.sum(gotstat[f, :, 1, :] + gotstat[f, :, 4, :], axis=0, keepdims=True)
        var = (spread + feat * jnp.sum(off * off, axis=0, keepdims=True)) * (1.0 / width)
        scale = jnp.transpose(jnp.broadcast_to(lax.rsqrt(var + 1e-06), (8, 128)))[0:tile, 0:1]
        lines = jnp.concatenate([gotstat[f, :, 2, :], gotstat[f, :, 5, :]], axis=0)
        fixed = jnp.dot(jnp.transpose(off), lines[:, 0:patch], precision=HIGH, preferred_element_type=F32)[0:tile]
        total_base = jnp.sum(lines, axis=0, keepdims=True)[:, patch:] + biasbuf[...].reshape(1, patch)
        summed = got[f, 0].astype(F32)
        for i in range(1, pairs):
            summed = summed + got[f, i].astype(F32)
        summed = jnp.concatenate([summed[:, :patch], summed[:, patch:]], axis=0)
        done = ((summed + fixed) * scale + total_base).astype(BF16).astype(F32)
        rows[f, 1] = jnp.concatenate([done[:half], done[half:]], axis=1).astype(BF16)

        @pl.when(me < num_dev - 1)
        def _():
            to_next(f).start()

        @pl.when(me > 0)
        def _():
            to_last(f).start()

        @pl.when(me == 0)
        def _():
            rows[f, 0] = jnp.zeros((half, 128), BF16)

        @pl.when(me == num_dev - 1)
        def _():
            rows[f, 2] = jnp.zeros((half, 128), BF16)

    def gather(f):
        @pl.when(me > 0)
        def _():
            to_next(f).wait_recv()

        @pl.when(me < num_dev - 1)
        def _():
            to_last(f).wait_recv()

        quads = []
        col = lax.broadcasted_iota(jnp.int32, (tile, 1), 0)
        for h in range(3):
            pair = rows[f, h].astype(F32)
            token = jnp.concatenate([pair[:, :patch], pair[:, patch:]], axis=0)
            before = jnp.where(col == 0, 0.0, pltpu.roll(token, 1, 0))
            after = jnp.where(col == tile - 1, 0.0, pltpu.roll(token, tile - 1, 0))
            for q in range(2):
                a = 2 * q * ch
                quads.append(jnp.concatenate(
                    [before[:, a + ch : a + 2 * ch], token[:, a : a + 2 * ch], after[:, a : a + ch]], axis=1))
        for i in range(4):
            x1_ref[f, i] = jnp.concatenate(quads[i : i + 3], axis=1).astype(BF16)

    merge(0)
    gather(0)
    stage_in(num_dev, me, 0, x1_ref, w1s, b1_ref, g1_ref, act1, edge1)
    stage_up(num_dev, me, act1, edge1, w2_ref, b2_ref, g2_ref, c2, act2)
    merge(1)
    m3 = (act2.shape[0] - 2) * TOK_W
    for s in (0, 2):
        for a in range(2):
            old = stage_out(act2, w3_ref, a, s // 2)
            for g in range(2):
                res_ref[pl.ds(4 * m3 * a + s + g, m3, stride=4), :] = old[:, g * 128 : (g + 1) * 128] + b3
    gather(1)

    for f in range(frames):
        for copy in swap(f) + messages(f):
            copy.wait_send()
        @pl.when(me < num_dev - 1)
        def _():
            to_next(f).wait_send()

        @pl.when(me > 0)
        def _():
            to_last(f).wait_send()


def local(
    hidden, mod_shift, mod_scale, head_weight, head_bias, conv_in_weight, conv_in_bias, gain_in,
    up_weight, up_bias, gain_up, out_weight, out_bias,
):
    num_dev = lax.axis_size("seq")
    frames, feat, tok_total = hidden.shape
    tile = tok_total // num_dev
    rows_dev = tile // TOK_W
    patch, width = head_weight.shape
    lat_ch, c1 = conv_in_weight.shape[3:]
    c2, c3 = out_weight.shape[3:]
    lat_rows = 2 * rows_dev
    window = min(width, (feat + 255 - math.gcd(feat, 128)) // 128 * 128)
    vmem = pl.BlockSpec(memory_space=pltpu.VMEM)
    hbm = pl.BlockSpec(memory_space=pltpu.HBM)
    half = tile // 2
    pairs = num_dev // 2
    raw = (hidden, head_weight, mod_scale[None], mod_shift[None], head_bias,
           jnp.transpose(up_weight, (0, 1, 3, 2)), out_weight, conv_in_weight,
           conv_in_bias, gain_in, up_bias, gain_up, out_bias)
    cells = frames * 2 * lat_rows * 4 * TOK_W
    act1 = pltpu.VMEM((lat_rows + 2, TOK_W, 3 * c1), BF16)
    edge1 = pltpu.VMEM((2, 16, 2 * c1), BF16)
    act2 = pltpu.VMEM((2 * lat_rows + 2, TOK_W, 3 * 384), BF16)
    made = pl.pallas_call(
        functools.partial(exchange_kernel, num_dev),
        out_shape=[
            jax.ShapeDtypeStruct((frames, lat_rows + 2, TOK_W, 12 * lat_ch), BF16),
            jax.ShapeDtypeStruct((2, 12 * lat_ch, 2 * c1), BF16),
            jax.ShapeDtypeStruct((2, 2 * c1, 768), BF16),
            jax.ShapeDtypeStruct((2, 3, 768, 256), BF16),
            jax.ShapeDtypeStruct((1, c1), F32),
            jax.ShapeDtypeStruct((1, c1), F32),
            jax.ShapeDtypeStruct((1, 256), F32),
            jax.ShapeDtypeStruct((1, 256), F32),
            jax.ShapeDtypeStruct((cells, 128), F32),
        ],
        in_specs=[hbm] * len(raw),
        out_specs=[vmem] * 9,
        scratch_shapes=[
            pltpu.VMEM((frames, feat, tok_total), BF16),
            pltpu.VMEM((patch, window), F32),
            pltpu.VMEM((2, 1, window), F32),
            pltpu.VMEM((3, 3, c2, c1), BF16),
            pltpu.VMEM((2, 3, 3, c2, c3), BF16),
            pltpu.VMEM((3, 3, 3, lat_ch, c1), BF16),
            pltpu.VMEM((patch,), F32),
            pltpu.VMEM((c1,), F32),
            pltpu.VMEM((c1,), F32),
            pltpu.VMEM((c2,), F32),
            pltpu.VMEM((c2,), F32),
            pltpu.VMEM((c3,), F32),
            act1,
            edge1,
            act2,
            pltpu.VMEM((frames, 2, pairs, half, 2 * patch), F32),
            pltpu.VMEM((frames, 2, pairs, 8, 128), F32),
            pltpu.VMEM((frames, pairs, half, 2 * patch), F32),
            pltpu.VMEM((frames, pairs, 8, 128), F32),
            pltpu.VMEM((frames, pairs, half, 2 * patch), BF16),
            pltpu.VMEM((frames, pairs, 8, 128), F32),
            pltpu.VMEM((frames, pairs, half, 2 * patch), BF16),
            pltpu.VMEM((frames, pairs, 8, 128), F32),
            pltpu.VMEM((frames, 3, half, 2 * patch), BF16),
            pltpu.SemaphoreType.DMA((5,)),
            pltpu.SemaphoreType.DMA((9,)),
            pltpu.SemaphoreType.DMA((frames, 2)),
            pltpu.SemaphoreType.DMA((frames, 2)),
            pltpu.SemaphoreType.DMA((frames, pairs)),
            pltpu.SemaphoreType.DMA((frames, pairs)),
            pltpu.SemaphoreType.DMA((frames, pairs)),
            pltpu.SemaphoreType.DMA((frames, pairs)),
            pltpu.SemaphoreType.DMA((frames, 2)),
            pltpu.SemaphoreType.DMA((frames, 2)),
        ],
        compiler_params=pltpu.CompilerParams(
            vmem_limit_bytes=26 * 1024 * 1024, collective_id=0, has_side_effects=True),
    )(*[pltpu.with_memory_space_constraint(value, pltpu.HBM) for value in raw])
    x1, w1s, w2, w3, b1, g1, b2, g2, res = made
    out = pl.pallas_call(
        functools.partial(conv_kernel, num_dev, c2),
        out_shape=jax.ShapeDtypeStruct((frames * 2 * lat_rows, c3, 4 * TOK_W), BF16),
        in_specs=[vmem] * 9,
        out_specs=hbm,
        scratch_shapes=[
            act1,
            edge1,
            act2,
            pltpu.VMEM((cells // 2, 128), F32),
            pltpu.VMEM((frames * 2 * lat_rows, c3, 4 * TOK_W), BF16),
            pltpu.SemaphoreType.DMA((frames * 2 * lat_rows,)),
        ],
        compiler_params=pltpu.CompilerParams(vmem_limit_bytes=26 * 1024 * 1024),
    )(x1, w1s, b1, g1, w2, b2, g2, w3, res)
    return out.reshape(frames, 2 * lat_rows, c3, 4 * TOK_W).transpose(0, 1, 3, 2)


def solution(mesh):
    placed = (P("grp", "seq", None), P(), P(), P(), P(), P(), P(), P(), P(), P(), P(), P(), P())
    return jax.shard_map(
        local, mesh=mesh, in_specs=placed, out_specs=P("grp", "seq", None, None), check_vma=False
    )
```

```python
import functools
import math

import jax
import jax.numpy as jnp
from jax import lax
from jax.experimental import pallas as pl
from jax.experimental.pallas import tpu as pltpu
from jax.sharding import PartitionSpec as P

TOK_W = 80
HIGH = lax.Precision.HIGHEST
F32 = jnp.float32
BF16 = jnp.bfloat16


def rms_silu(values, gain_vec):
    squares = jnp.mean(values * values, axis=-1, keepdims=True)
    normed = values * lax.rsqrt(squares + 1e-06) * gain_vec
    return normed * jax.nn.sigmoid(normed)


def shift_cols(values, step):
    count = values.shape[0]
    col = lax.broadcasted_iota(jnp.int32, (count, 1), 0) % TOK_W
    if step > 0:
        return jnp.where(col == 0, 0.0, pltpu.roll(values, 1, 0))
    return jnp.where(col == TOK_W - 1, 0.0, pltpu.roll(values, count - 1, 0))


def inside(count, first, step, total):
    row = lax.broadcasted_iota(jnp.int32, (count, 1), 0) // TOK_W * step + first
    return (row >= 0) & (row < total)


def stage_in(num_dev, dev, frame, x_ref, w1s, b1_ref, g1_ref, act1, edge1):
    rows1 = x_ref.shape[1]
    lat_rows = rows1 - 2
    c1 = g1_ref.shape[1]
    m1 = rows1 * TOK_W
    keep1 = inside(m1, dev * lat_rows - 1, 1, num_dev * lat_rows)
    x_now = x_ref[frame].reshape(m1, x_ref.shape[-1])
    pre = jnp.dot(x_now, w1s[1], preferred_element_type=F32)
    if frame == 1:
        x_old = x_ref[0].reshape(m1, x_ref.shape[-1])
        pre = pre + jnp.dot(x_old, w1s[0], preferred_element_type=F32)
    for r in range(2):
        val = rms_silu(pre[:, r * c1 : (r + 1) * c1] + b1_ref[...], g1_ref[...])
        val = jnp.where(keep1, val, 0.0)
        act1[:, :, r * c1 : (r + 1) * c1] = val.astype(BF16).reshape(rows1, TOK_W, c1)
        if r == 0:
            moved = shift_cols(val, -1)
            act1[:, :, 2 * c1 : 3 * c1] = moved.astype(BF16).reshape(rows1, TOK_W, c1)
            firsts = [val[i * TOK_W : i * TOK_W + 1] for i in range(rows1)]
            fill = [jnp.zeros((17 - rows1, c1), F32)]
            for k in range(2):
                edge1[k, :, 0:c1] = jnp.zeros((16, c1), BF16)
                edge1[k, :, c1 : 2 * c1] = jnp.concatenate(firsts[k : k + rows1 - 1] + fill, axis=0).astype(BF16)


def silu(values):
    return values * jax.nn.sigmoid(values)


def stage_up(num_dev, dev, act1, edge1, w2_ref, b2_ref, g2_ref, chans, act2):
    rows2 = act1.shape[0] - 1
    lat_rows = rows2 - 1
    c1 = act1.shape[2] // 3
    m2 = rows2 * TOK_W
    left = lax.broadcasted_iota(jnp.int32, (1, 128), 1) < chans - 128
    for t in range(2):
        lanes = slice(t * c1, (t + 2) * c1)
        top = act1[0:rows2, :, lanes].reshape(m2, 2 * c1)
        low = act1[1 : rows2 + 1, :, lanes].reshape(m2, 2 * c1)
        if t == 1:
            top = jnp.concatenate([top, edge1[0]], axis=0)
            low = jnp.concatenate([low, edge1[1]], axis=0)
        count = top.shape[0]
        pre = jnp.dot(top, w2_ref[0], preferred_element_type=F32)
        pre = pre + jnp.dot(low, w2_ref[1], preferred_element_type=F32)
        index = lax.broadcasted_iota(jnp.int32, (count, 1), 0)
        row = jnp.where(index < m2, index // TOK_W, index - m2)
        for p in range(2):
            a = pre[:, p * 384 : p * 384 + 128] + b2_ref[:, 0:128]
            b = pre[:, p * 384 + 128 : p * 384 + 256] + b2_ref[:, 0:128]
            h = pre[:, p * 384 + 256 : p * 384 + 384] + b2_ref[:, 128:256]
            sq = h * h
            sum_a = jnp.sum(a * a + jnp.where(left, sq, 0.0), axis=-1, keepdims=True)
            sum_b = jnp.sum(b * b + jnp.where(left, 0.0, sq), axis=-1, keepdims=True)
            inv_a = lax.rsqrt(sum_a * (1.0 / chans) + 1e-06)
            inv_b = lax.rsqrt(sum_b * (1.0 / chans) + 1e-06)
            line = 2 * dev * lat_rows + 2 * row - p
            keep = (line >= 0) & (line < 2 * num_dev * lat_rows)
            keep_a, keep_b = keep, keep
            if t == 1:
                keep_a = keep & (index < m2)
                keep_b = keep & ((index >= m2) | (index % TOK_W != TOK_W - 1))
            gain_a = jnp.where(keep_a, inv_a, 0.0)
            gain_b = jnp.where(keep_b, inv_b, 0.0)
            a = silu(a * gain_a * g2_ref[:, 0:128])
            b = silu(b * gain_b * g2_ref[:, 0:128])
            h = silu(h * jnp.where(left, gain_a, gain_b) * g2_ref[:, 128:256])
            val = jnp.concatenate([a, b, h], axis=1)
            main = val[0:m2]
            piece = main.astype(BF16).reshape(rows2, TOK_W, 384)
            for i in range(rows2):
                act2[2 * i + 1 - p, :, (t + 1) * 384 : (t + 2) * 384] = piece[i]
            if t == 1:
                moved = pltpu.roll(main, 1, 0)
                col = lax.broadcasted_iota(jnp.int32, (TOK_W, 1), 0)
                for i in range(rows2):
                    block = jnp.where(col == 0, val[m2 + i : m2 + i + 1], moved[i * TOK_W : (i + 1) * TOK_W])
                    act2[2 * i + 1 - p, :, 0:384] = block.astype(BF16)


def stage_out(act2, w3_ref, part, t):
    rows3 = act2.shape[0] - 2
    total = None
    for b in range(3):
        block = act2[b : b + rows3, :, t * 384 : t * 384 + 768].reshape(rows3 * TOK_W, 768)
        one = jnp.dot(block, w3_ref[part, b], preferred_element_type=F32)
        total = one if total is None else total + one
    return total


def conv_kernel(num_dev, chans, x_ref, w1s, b1_ref, g1_ref, w2_ref, b2_ref, g2_ref, w3_ref, res_ref, out_hbm,
                act1, edge1, act2, res, obuf, out_sem):
    dev = lax.axis_index("seq")
    rows3 = act2.shape[0] - 2
    m3 = rows3 * TOK_W
    c3 = obuf.shape[1]
    width = 4 * TOK_W
    copies = [pltpu.make_async_copy(obuf.at[i], out_hbm.at[i], out_sem.at[i]) for i in range(2 * rows3)]
    stage_in(num_dev, dev, 1, x_ref, w1s, b1_ref, g1_ref, act1, edge1)
    for i in range(rows3):
        obuf[i] = jnp.transpose(res_ref[i * width : (i + 1) * width, :])[0:c3].astype(BF16)
        copies[i].start()
    stage_up(num_dev, dev, act1, edge1, w2_ref, b2_ref, g2_ref, chans, act2)
    for s in (0, 2):
        new = stage_out(act2, w3_ref, 0, s // 2)
        for g in range(2):
            old = res_ref[pl.ds(4 * m3 + s + g, m3, stride=4), :]
            res[pl.ds(s + g, m3, stride=4), :] = new[:, g * 128 : (g + 1) * 128] + old
    for i in range(rows3):
        obuf[rows3 + i] = jnp.transpose(res[i * width : (i + 1) * width, :])[0:c3].astype(BF16)
        copies[rows3 + i].start()
    for copy in copies:
        copy.wait()


def exchange_kernel(num_dev, x_hbm, w_hbm, scale_hbm, shift_hbm, bias_hbm, up_hbm, outw_hbm, w1_hbm,
                    b1_hbm, g1_hbm, b2_hbm, g2_hbm, b3_hbm,
                    x1_ref, w1s, w2_ref, w3_ref, b1_ref, g1_ref, b2_ref, g2_ref, res_ref,
                    xbuf, wbuf, modbuf, upbuf, outbuf, w1buf, biasbuf, b1buf, g1buf, b2buf, g2buf, b3buf, act1, edge1, act2, pair, pairstat, gotpair, gotpairstat, send, stat, got, gotstat, rows,
                    in_sem, weight_sem, pair_send, pair_recv, send_sem, recv_sem, stat_send, stat_recv, halo_send, halo_recv):
    frames, feat, total = x_hbm.shape
    patch, width = w_hbm.shape
    tile = total // num_dev
    half = tile // 2
    c1, c2 = up_hbm.shape[3], up_hbm.shape[2]
    c3 = outw_hbm.shape[4]
    me = lax.axis_index("seq")

    def peer(step):
        spot = me
        bit = 1
        while bit < num_dev:
            if step & bit:
                spot = spot + (1 - 2 * ((me // bit) % 2)) * bit
            bit *= 2
        return spot

    window = wbuf.shape[1]
    begin = jnp.minimum((me * feat) // 128 * 128, width - window)
    lanes = pl.ds(pl.multiple_of(begin, 128), window)
    loads = [
        pltpu.make_async_copy(w_hbm.at[:, lanes], wbuf, in_sem.at[0]),
        pltpu.make_async_copy(scale_hbm.at[:, lanes], modbuf.at[0], in_sem.at[1]),
        pltpu.make_async_copy(shift_hbm.at[:, lanes], modbuf.at[1], in_sem.at[2]),
    ]
    planes = [pltpu.make_async_copy(x_hbm.at[f], xbuf.at[f], in_sem.at[3 + f]) for f in range(frames)]
    weights = [
        pltpu.make_async_copy(up_hbm, upbuf, weight_sem.at[0]),
        pltpu.make_async_copy(outw_hbm.at[pl.ds(1, 2)], outbuf, weight_sem.at[1]),
        pltpu.make_async_copy(bias_hbm, biasbuf, weight_sem.at[2]),
        pltpu.make_async_copy(b1_hbm, b1buf, weight_sem.at[3]),
        pltpu.make_async_copy(g1_hbm, g1buf, weight_sem.at[4]),
        pltpu.make_async_copy(b3_hbm, b3buf, weight_sem.at[5]),
        pltpu.make_async_copy(w1_hbm, w1buf, weight_sem.at[6]),
        pltpu.make_async_copy(b2_hbm, b2buf, weight_sem.at[7]),
        pltpu.make_async_copy(g2_hbm, g2buf, weight_sem.at[8]),
    ]
    for copy in planes[:1] + loads + planes[1:]:
        copy.start()

    barrier = pltpu.get_barrier_semaphore()
    for step in range(1, num_dev):
        pl.semaphore_signal(barrier, inc=1, device_id={"seq": peer(step)})

    for copy in loads:
        copy.wait()
    turn = lax.rem(begin - me * feat + window, window)
    plain = pltpu.roll(wbuf[...], turn, 1)[:, 0:feat]
    scale = pltpu.roll(jnp.broadcast_to(modbuf[0], (8, window)), turn, 1)[0:1, 0:feat]
    shift = pltpu.roll(jnp.broadcast_to(modbuf[1], (8, window)), turn, 1)[0:1, 0:feat]
    weight = plain * (1.0 + scale)
    high = weight.astype(BF16)
    low = (weight - high.astype(F32)).astype(BF16)
    stack = jnp.concatenate([high, low], axis=0)
    sums = jnp.sum(high.astype(F32) + low.astype(F32), axis=1, keepdims=True)
    base = jnp.sum(plain * shift, axis=1, keepdims=True)
    both = jnp.concatenate([sums, base], axis=0)
    line = jnp.transpose(jnp.broadcast_to(both, (2 * patch, 8)))

    core = lax.rem(me, 2)
    mine = me // 2
    pairs = num_dev // 2

    def swap(f):
        return [
            pltpu.make_async_remote_copy(
                src_ref=pairstat.at[f, 1 - core], dst_ref=gotpairstat.at[f], send_sem=pair_send.at[f, 0],
                recv_sem=pair_recv.at[f, 0], device_id={"seq": peer(1)}),
            pltpu.make_async_remote_copy(
                src_ref=pair.at[f, 1 - core], dst_ref=gotpair.at[f], send_sem=pair_send.at[f, 1],
                recv_sem=pair_recv.at[f, 1], device_id={"seq": peer(1)}),
        ]

    def transfer(f, other, slot):
        return [
            pltpu.make_async_remote_copy(
                src_ref=stat.at[f, other // 2], dst_ref=gotstat.at[f, slot], send_sem=stat_send.at[f, other // 2],
                recv_sem=stat_recv.at[f, slot], device_id={"seq": other}),
            pltpu.make_async_remote_copy(
                src_ref=send.at[f, other // 2], dst_ref=got.at[f, slot], send_sem=send_sem.at[f, other // 2],
                recv_sem=recv_sem.at[f, slot], device_id={"seq": other}),
        ]

    def messages(f):
        out = []
        for step in range(num_dev - 2, 0, -2):
            out += transfer(f, peer(step), mine)
        return out

    def arrivals(f):
        out = []
        for step in range(num_dev - 2, 0, -2):
            out += transfer(f, peer(step), peer(step) // 2)
        return out

    for f in range(frames):
        planes[f].wait()
        if f == 0:
            for copy in weights:
                copy.start()
        block = xbuf[f]
        full = jnp.dot(stack, block, preferred_element_type=F32)
        values = block.astype(F32)
        mean = jnp.sum(values, axis=0, keepdims=True) * (1.0 / feat)
        centred = values - mean
        spread = jnp.sum(centred * centred, axis=0, keepdims=True)
        part = full[:patch] + full[patch:] - sums * mean
        flat = jnp.transpose(part).reshape(pairs, 2, 2, half, patch)
        for c in range(2):
            pair[f, c] = jnp.concatenate([flat[:, c, 0], flat[:, c, 1]], axis=-1)
            for i in range(pairs):
                at = slice((2 * i + c) * tile, (2 * i + c + 1) * tile)
                pairstat[f, c, i, 0:1, 0:tile] = mean[:, at]
                pairstat[f, c, i, 1:2, 0:tile] = spread[:, at]
                pairstat[f, c, i, 2:3, :] = line[0:1]
                pairstat[f, c, i, 3:8, :] = jnp.zeros((5, 128), F32)
        if f == 0:
            pl.semaphore_wait(barrier, num_dev - 1)
        for copy in swap(f):
            copy.start()
    for f in range(frames):
        for copy in swap(f):
            copy.wait_recv()
        send[f] = (pair[f, core] + gotpair[f]).astype(BF16)
        stat[f, :, 0:3, :] = pairstat[f, core, :, 0:3, :]
        stat[f, :, 3:6, :] = gotpairstat[f, :, 0:3, :]
        for copy in messages(f):
            copy.start()
        got[f, mine] = send[f, mine]
        gotstat[f, mine] = stat[f, mine]

    for copy in weights:
        copy.wait()
    taps = [[jnp.transpose(upbuf[r, c].astype(F32)) for c in range(3)] for r in range(3)]
    for p in range(2):
        for i in range(2):
            group = ((0,), (1, 2)) if p == 0 else ((0, 1), (2,))
            tall = [functools.reduce(lambda a, b: a + b, [taps[r][c] for r in group[i]]) for c in range(3)]
            for q in range(2):
                first = tall[0] if q == 0 else tall[0] + tall[1]
                second = tall[1] + tall[2] if q == 0 else tall[2]
                for k, half_w in enumerate((first, second)):
                    down = slice(k * c1, (k + 1) * c1)
                    lo = p * 384 + (1 - q) * 128
                    hi = p * 384 + 256 + (1 - q) * (c2 - 128)
                    w2_ref[i, down, lo : lo + 128] = half_w[:, 0:128].astype(BF16)
                    w2_ref[i, down, hi : hi + c2 - 128] = half_w[:, 128:c2].astype(BF16)
    w3_ref[...] = jnp.zeros(w3_ref.shape, BF16)
    b1_ref[...] = b1buf[...].reshape(1, c1)
    g1_ref[...] = g1buf[...].reshape(1, c1)
    b2 = b2buf[...].reshape(1, c2)
    g2 = g2buf[...].reshape(1, c2)
    b2_ref[...] = jnp.concatenate([b2, b2[:, 128:c2]], axis=1)
    g2_ref[...] = jnp.concatenate([g2, g2[:, 128:c2]], axis=1)
    b3 = jnp.concatenate([b3buf[...].reshape(1, c3), jnp.zeros((1, 128 - c3), F32)], axis=1)
    ch = patch // 4
    blank = jnp.zeros((ch, c1), BF16)
    for a in range(2):
        for b in range(3):
            for j in range(4):
                spot = slice((4 * b + j) * ch, (4 * b + j + 1) * ch)
                w1s[a, spot, 0:c1] = w1buf[a + 1, b, j] if j < 3 else blank
                w1s[a, spot, c1 : 2 * c1] = w1buf[a + 1, b, j - 1] if j > 0 else blank
    for b in range(3):
        for e in range(3):
            for a in range(2):
                for g in range(2):
                    k = e + g
                    lo = k // 2 * 384 + k % 2 * 128
                    hi = k // 2 * 384 + 256 + k % 2 * (c2 - 128)
                    w3_ref[a, b, lo : lo + 128, g * 128 : g * 128 + c3] = outbuf[1 - a, b, e, 0:128, :]
                    w3_ref[a, b, hi : hi + c2 - 128, g * 128 : g * 128 + c3] = outbuf[1 - a, b, e, 128:c2, :]

    def to_next(f):
        return pltpu.make_async_remote_copy(
            src_ref=rows.at[f, 1], dst_ref=rows.at[f, 0], send_sem=halo_send.at[f, 0],
            recv_sem=halo_recv.at[f, 0], device_id={"seq": lax.rem(me + 1, num_dev)})

    def to_last(f):
        return pltpu.make_async_remote_copy(
            src_ref=rows.at[f, 1], dst_ref=rows.at[f, 2], send_sem=halo_send.at[f, 1],
            recv_sem=halo_recv.at[f, 1], device_id={"seq": lax.rem(me + num_dev - 1, num_dev)})

    def merge(f):
        for copy in arrivals(f):
            copy.wait_recv()
        means = jnp.concatenate([gotstat[f, :, 0, :], gotstat[f, :, 3, :]], axis=0)
        off = means - jnp.mean(means, axis=0, keepdims=True)
        spread = jnp.sum(gotstat[f, :, 1, :] + gotstat[f, :, 4, :], axis=0, keepdims=True)
        var = (spread + feat * jnp.sum(off * off, axis=0, keepdims=True)) * (1.0 / width)
        scale = jnp.transpose(jnp.broadcast_to(lax.rsqrt(var + 1e-06), (8, 128)))[0:tile, 0:1]
        lines = jnp.concatenate([gotstat[f, :, 2, :], gotstat[f, :, 5, :]], axis=0)
        fixed = jnp.dot(jnp.transpose(off), lines[:, 0:patch], precision=HIGH, preferred_element_type=F32)[0:tile]
        total_base = jnp.sum(lines, axis=0, keepdims=True)[:, patch:] + biasbuf[...].reshape(1, patch)
        summed = got[f, 0].astype(F32)
        for i in range(1, pairs):
            summed = summed + got[f, i].astype(F32)
        summed = jnp.concatenate([summed[:, :patch], summed[:, patch:]], axis=0)
        done = ((summed + fixed) * scale + total_base).astype(BF16).astype(F32)
        rows[f, 1] = jnp.concatenate([done[:half], done[half:]], axis=1).astype(BF16)

        @pl.when(me < num_dev - 1)
        def _():
            to_next(f).start()

        @pl.when(me > 0)
        def _():
            to_last(f).start()

        @pl.when(me == 0)
        def _():
            rows[f, 0] = jnp.zeros((half, 128), BF16)

        @pl.when(me == num_dev - 1)
        def _():
            rows[f, 2] = jnp.zeros((half, 128), BF16)

    def gather(f):
        @pl.when(me > 0)
        def _():
            to_next(f).wait_recv()

        @pl.when(me < num_dev - 1)
        def _():
            to_last(f).wait_recv()

        quads = []
        col = lax.broadcasted_iota(jnp.int32, (tile, 1), 0)
        for h in range(3):
            pair = rows[f, h].astype(F32)
            token = jnp.concatenate([pair[:, :patch], pair[:, patch:]], axis=0)
            before = jnp.where(col == 0, 0.0, pltpu.roll(token, 1, 0))
            after = jnp.where(col == tile - 1, 0.0, pltpu.roll(token, tile - 1, 0))
            for q in range(2):
                a = 2 * q * ch
                quads.append(jnp.concatenate(
                    [before[:, a + ch : a + 2 * ch], token[:, a : a + 2 * ch], after[:, a : a + ch]], axis=1))
        for i in range(4):
            x1_ref[f, i] = jnp.concatenate(quads[i : i + 3], axis=1).astype(BF16)

    merge(0)
    gather(0)
    stage_in(num_dev, me, 0, x1_ref, w1s, b1_ref, g1_ref, act1, edge1)
    stage_up(num_dev, me, act1, edge1, w2_ref, b2_ref, g2_ref, c2, act2)
    merge(1)
    m3 = (act2.shape[0] - 2) * TOK_W
    for s in (0, 2):
        for a in range(2):
            old = stage_out(act2, w3_ref, a, s // 2)
            for g in range(2):
                res_ref[pl.ds(4 * m3 * a + s + g, m3, stride=4), :] = old[:, g * 128 : (g + 1) * 128] + b3
    gather(1)

    for f in range(frames):
        for copy in swap(f) + messages(f):
            copy.wait_send()
        @pl.when(me < num_dev - 1)
        def _():
            to_next(f).wait_send()

        @pl.when(me > 0)
        def _():
            to_last(f).wait_send()


def local(
    hidden, mod_shift, mod_scale, head_weight, head_bias, conv_in_weight, conv_in_bias, gain_in,
    up_weight, up_bias, gain_up, out_weight, out_bias,
):
    num_dev = lax.axis_size("seq")
    frames, feat, tok_total = hidden.shape
    tile = tok_total // num_dev
    rows_dev = tile // TOK_W
    patch, width = head_weight.shape
    lat_ch, c1 = conv_in_weight.shape[3:]
    c2, c3 = out_weight.shape[3:]
    lat_rows = 2 * rows_dev
    window = min(width, (feat + 255 - math.gcd(feat, 128)) // 128 * 128)
    vmem = pl.BlockSpec(memory_space=pltpu.VMEM)
    hbm = pl.BlockSpec(memory_space=pltpu.HBM)
    half = tile // 2
    pairs = num_dev // 2
    raw = (hidden, head_weight, mod_scale[None], mod_shift[None], head_bias,
           jnp.transpose(up_weight, (0, 1, 3, 2)), out_weight, conv_in_weight,
           conv_in_bias, gain_in, up_bias, gain_up, out_bias)
    cells = frames * 2 * lat_rows * 4 * TOK_W
    act1 = pltpu.VMEM((lat_rows + 2, TOK_W, 3 * c1), BF16)
    edge1 = pltpu.VMEM((2, 16, 2 * c1), BF16)
    act2 = pltpu.VMEM((2 * lat_rows + 2, TOK_W, 3 * 384), BF16)
    made = pl.pallas_call(
        functools.partial(exchange_kernel, num_dev),
        out_shape=[
            jax.ShapeDtypeStruct((frames, lat_rows + 2, TOK_W, 12 * lat_ch), BF16),
            jax.ShapeDtypeStruct((2, 12 * lat_ch, 2 * c1), BF16),
            jax.ShapeDtypeStruct((2, 2 * c1, 768), BF16),
            jax.ShapeDtypeStruct((2, 3, 768, 256), BF16),
            jax.ShapeDtypeStruct((1, c1), F32),
            jax.ShapeDtypeStruct((1, c1), F32),
            jax.ShapeDtypeStruct((1, 256), F32),
            jax.ShapeDtypeStruct((1, 256), F32),
            jax.ShapeDtypeStruct((cells, 128), F32),
        ],
        in_specs=[hbm] * len(raw),
        out_specs=[vmem] * 9,
        scratch_shapes=[
            pltpu.VMEM((frames, feat, tok_total), BF16),
            pltpu.VMEM((patch, window), F32),
            pltpu.VMEM((2, 1, window), F32),
            pltpu.VMEM((3, 3, c2, c1), BF16),
            pltpu.VMEM((2, 3, 3, c2, c3), BF16),
            pltpu.VMEM((3, 3, 3, lat_ch, c1), BF16),
            pltpu.VMEM((patch,), F32),
            pltpu.VMEM((c1,), F32),
            pltpu.VMEM((c1,), F32),
            pltpu.VMEM((c2,), F32),
            pltpu.VMEM((c2,), F32),
            pltpu.VMEM((c3,), F32),
            act1,
            edge1,
            act2,
            pltpu.VMEM((frames, 2, pairs, half, 2 * patch), F32),
            pltpu.VMEM((frames, 2, pairs, 8, 128), F32),
            pltpu.VMEM((frames, pairs, half, 2 * patch), F32),
            pltpu.VMEM((frames, pairs, 8, 128), F32),
            pltpu.VMEM((frames, pairs, half, 2 * patch), BF16),
            pltpu.VMEM((frames, pairs, 8, 128), F32),
            pltpu.VMEM((frames, pairs, half, 2 * patch), BF16),
            pltpu.VMEM((frames, pairs, 8, 128), F32),
            pltpu.VMEM((frames, 3, half, 2 * patch), BF16),
            pltpu.SemaphoreType.DMA((5,)),
            pltpu.SemaphoreType.DMA((9,)),
            pltpu.SemaphoreType.DMA((frames, 2)),
            pltpu.SemaphoreType.DMA((frames, 2)),
            pltpu.SemaphoreType.DMA((frames, pairs)),
            pltpu.SemaphoreType.DMA((frames, pairs)),
            pltpu.SemaphoreType.DMA((frames, pairs)),
            pltpu.SemaphoreType.DMA((frames, pairs)),
            pltpu.SemaphoreType.DMA((frames, 2)),
            pltpu.SemaphoreType.DMA((frames, 2)),
        ],
        compiler_params=pltpu.CompilerParams(
            vmem_limit_bytes=26 * 1024 * 1024, collective_id=0, has_side_effects=True),
    )(*[pltpu.with_memory_space_constraint(value, pltpu.HBM) for value in raw])
    x1, w1s, w2, w3, b1, g1, b2, g2, res = made
    out = pl.pallas_call(
        functools.partial(conv_kernel, num_dev, c2),
        out_shape=jax.ShapeDtypeStruct((frames * 2 * lat_rows, c3, 4 * TOK_W), BF16),
        in_specs=[vmem] * 9,
        out_specs=hbm,
        scratch_shapes=[
            act1,
            edge1,
            act2,
            pltpu.VMEM((cells // 2, 128), F32),
            pltpu.VMEM((frames * 2 * lat_rows, c3, 4 * TOK_W), BF16),
            pltpu.SemaphoreType.DMA((frames * 2 * lat_rows,)),
        ],
        compiler_params=pltpu.CompilerParams(vmem_limit_bytes=26 * 1024 * 1024),
    )(x1, w1s, b1, g1, w2, b2, g2, w3, res)
    return out.reshape(frames, 2 * lat_rows, c3, 4 * TOK_W).transpose(0, 1, 3, 2)


def solution(mesh):
    placed = (P("grp", "seq", None), P(), P(), P(), P(), P(), P(), P(), P(), P(), P(), P(), P())
    return jax.shard_map(
        local, mesh=mesh, in_specs=placed, out_specs=P("grp", "seq", None, None), check_vma=False
    )
```
